32 devices in a mesh: groups: 2 (over x), seq: 8 (over z, y), exp: 2 (over core).
Axes of the slice: x: 2, y: 2, z: 4, core: 2. Of those that a mesh axis runs over, the one named last changes fastest.
Arguments:
- queries: bfloat16 [4096, 2048], P(('groups', 'seq'), 'exp'), parts along dimension 0, may hold values from -6 to 6
- key_rows: bfloat16 [4096, 256], P(('groups', 'seq'), 'exp'), parts along dimension 0, may hold values from -6 to 6
- values: bfloat16 [4096, 256], P(('groups', 'seq'), 'exp'), parts along dimension 0, may hold values from -6 to 6
- sink_logit: float32 [32], P('exp'), may hold values from 0 to 5
- o_weight: bfloat16 [2048, 1440], P('exp'), may hold values from -0.5 to 0.5
- residual: bfloat16 [4096, 1440], P(('groups', 'seq')), parts along dimension 0, may hold values from -30 to 30
- norm_gain: float32 [1440], replicated, may hold values from 0.1 to 1.9
- routes: int32 [4096, 4], P(('groups', 'seq')), parts along dimension 0, may hold values from 0 to 7, all different within a row; in each aligned block of 128 rows (0 to 127, 128 to 255, ...) at most 128 rows name the same one
- gate_codes: int32 [4096, 4], P(('groups', 'seq')), parts along dimension 0, may hold values from 1 to 256
- w_gate: bfloat16 [8, 1440, 1440], P('seq', None, 'exp'), may hold values from -0.15625 to 0.15625
- w_up: bfloat16 [8, 1440, 1440], P('seq', None, 'exp'), may hold values from -0.15625 to 0.15625
- w_down: bfloat16 [8, 1440, 1440], P('seq', 'exp'), may hold values from -0.15625 to 0.15625
Outputs:
- attended: bfloat16 [4096, 1440], P(('groups', 'seq', 'exp')), parts along dimension 0
- expert_mix: bfloat16 [4096, 1440], P(('groups', 'seq', 'exp')), parts along dimension 0
The draws below stay inside these ranges and needn't reach their ends.
There are 2 independent parts, one for each index of `groups`. The reference program is written for one: setup_inputs(seed, part) draws one part's arguments, and reference() takes and returns one part's arrays. A program takes and returns all parts, laid end to end along the dimension named above; an argument that names none is the same for every part. Nothing has to cross between parts.
Inputs may be any that keep to these rules, and one draw needn't show every extreme that they name: `routes`: each row names 4 different experts; in each aligned block of 128 rows no expert is named by more than 128 rows, and in some block one expert is named by exactly 128 rows.
All inputs are finite; a program needn't handle non-finite values.
Results may differ from the reference program's by a relative error of at most 0.013.
Values may be sent and summed in bfloat16 or wider, within the bound.
A program may use at most 128 MiB of HBM per device.

```python
import math
import jax
import jax.numpy as jnp
import numpy as np
from jax import lax

D = 1440
HEADS = 32
KV_HEADS = 4
HEAD_DIM = 64
WINDOW = 128
FF = 1440
TOP = 4
TOK_DEV = 256
TOKENS = 2048
EXPERTS = 8
ROWS_DEV = 128
CAP = 128


def pair_draw(key):
    query_key = jax.random.fold_in(key, 101)
    kv_key = jax.random.fold_in(key, 102)
    query_vals = jnp.clip(jax.random.normal(query_key, (TOKENS, HEADS * HEAD_DIM), jnp.float32), -4.0, 4.0)
    key_vals = jnp.clip(jax.random.normal(kv_key, (TOKENS, KV_HEADS * HEAD_DIM), jnp.float32), -4.0, 4.0)
    return (query_vals, key_vals)


def draw_queries(key, part):
    return pair_draw(key)[0].astype(jnp.bfloat16)


def draw_key_rows(key, part):
    return pair_draw(key)[1].astype(jnp.bfloat16)


def draw_residual(key, part):
    base_key = jax.random.fold_in(key, 201)
    row_key = jax.random.fold_in(key, 202)
    col_key = jax.random.fold_in(key, 203)
    base = jax.random.normal(base_key, (TOKENS, D), jnp.float32)
    row_scale = jnp.exp(jax.random.uniform(row_key, (TOKENS, 1), jnp.float32, jnp.log(0.3), jnp.log(3.0)))
    col_scale = jnp.exp(jax.random.uniform(col_key, (1, D), jnp.float32, jnp.log(0.3), jnp.log(3.0)))
    return jnp.clip(base * row_scale * col_scale, -30.0, 30.0).astype(jnp.bfloat16)


def touch_ends(values, rng, smallest, high):
    index_at = [jax.random.randint(jax.random.fold_in(rng, axis), (), 0, length) for axis, length in enumerate(values.shape)]
    widest = values.shape.index(max(values.shape))
    beside = index_at[:widest] + [(index_at[widest] + 1) % values.shape[widest]] + index_at[widest + 1:]
    return values.at[tuple(index_at)].set(smallest).at[tuple(beside)].set(high)


def block_scale(stream_key, extent, split, smallest, high):
    def one(axis_at, parts):
        draws = jax.random.uniform(jax.random.fold_in(jax.random.fold_in(stream_key, 6), axis_at), (parts,), jnp.float32, smallest / len(split), high / len(split))
        return jnp.repeat(jnp.exp(draws), extent[axis_at] // parts).reshape((-1,) + (1,) * (len(extent) - axis_at - 1))

    factor_of = one(*split[0])
    for cut in split[1:]:
        factor_of = factor_of * one(*cut)
    return factor_of


def shared_out(stream_key, own, number, rows, number_of, top, reach, slope):
    order = jax.random.permutation(stream_key, number_of)
    packed, ordinary = load_shares(number_of, rows * top, reach, slope, True), load_shares(number_of, rows * top, reach, slope, False)
    places = jnp.arange(number_of)

    def named(sizes, turn):
        used = int((sizes > 0).sum())
        fixed = max(1, used // 4)
        passed = fixed + (places - fixed + turn * (used - fixed)) % max(1, number_of - fixed)
        return jnp.zeros((number_of,), jnp.int32).at[order[jnp.where(places < fixed, places, passed)]].set(jnp.asarray(sizes, jnp.int32))

    sizes = jnp.where(number % 4 == 0, named(packed, number // 4), named(ordinary, number - number // 4 - 1))
    mixed = jax.random.permutation(jax.random.fold_in(own, 3), number_of)
    donor, taker = mixed[0:number_of // 2 * 2:2], mixed[1:number_of // 2 * 2:2]
    margin = jnp.minimum(sizes[donor] - 1, reach - sizes[taker]) // 2
    margin = jnp.where((donor == order[0]) | (taker == order[0]) | (sizes[taker] == 0), 0, jnp.maximum(margin, 0))
    passed = jax.random.randint(jax.random.fold_in(own, 4), (number_of // 2,), 0, 1 << 20) % (margin + 1)
    sizes = sizes.at[donor].add(-passed).at[taker].add(passed)
    labels = jnp.searchsorted(jnp.cumsum(sizes), jnp.arange(rows * top), side="right").astype(jnp.int32)
    table = labels.reshape(top, rows).T
    table = table[jax.random.permutation(jax.random.fold_in(own, 1), rows)]
    turn = jax.random.randint(jax.random.fold_in(own, 2), (rows, 1), 0, top)
    return jnp.take_along_axis(table, (jnp.arange(top)[None, :] + turn) % top, axis=1)


def load_shares(amount, total, bound, skew, full):
    weights = [(1 << 20) // math.isqrt(rank ** skew) + 1 for rank in range(1, amount + 1)]
    largest = bound if full else min(bound, max(-(-total // amount), total * weights[0] // sum(weights)))
    least = 1 if total - largest >= amount - 1 else 0
    holding, rest = [largest] + [least] * (amount - 1), total - largest - least * (amount - 1)
    while rest > 0:
        candidates = [i for i in range(1, amount) if holding[i] < largest] or [i for i in range(1, amount) if holding[i] < bound]
        pool, remaining = sum([weights[i] for i in candidates]), rest
        for i in candidates:
            extra = min(bound - holding[i], max(1, remaining * weights[i] // pool), rest)
            holding[i] = holding[i] + extra
            rest = rest - extra
    return np.array(holding)


def scatter_about(key, dims, scale, reach, shards=(), held_as=jnp.bfloat16):
    gain = block_scale(key, dims, shards, -0.22, 0.18) if shards else 1.0
    values = jax.random.normal(key, dims, jnp.float32) * scale * gain
    return jnp.minimum(jnp.maximum(values, -reach), reach).astype(held_as)


def setup_inputs(seed: int = 0, part: int = 0) -> dict:
    arg_keys = jax.random.split(jax.random.key(seed), 13)
    part_splits = jax.random.split(jax.random.fold_in(arg_keys[12], part), 13)
    queries = draw_queries(jax.random.fold_in(jax.random.fold_in(arg_keys[12], part), 71), part)
    key_rows = draw_key_rows(jax.random.fold_in(jax.random.fold_in(arg_keys[12], part), 71), part)
    values = scatter_about(part_splits[2], (TOKENS, KV_HEADS * HEAD_DIM), 1.0, 6.0, ((0, 8), (1, 2)))
    sink_logit = jnp.clip(5.0 * jax.random.uniform(arg_keys[3], (HEADS,), jnp.float32) ** block_scale(arg_keys[3], (HEADS,), ((0, 2),), -0.2, 0.2), 0.0, 5.0)
    o_weight = scatter_about(arg_keys[4], (HEADS * HEAD_DIM, D), (HEADS * HEAD_DIM // 16) ** -0.5, 0.5, ((0, 2),))
    residual = draw_residual(jax.random.fold_in(jax.random.fold_in(arg_keys[12], part), 71), part)
    norm_gain = jnp.clip(1.0 + 0.18 * jax.random.normal(arg_keys[6], (D,), jnp.float32), 0.1, 1.9)
    routes_keys = jax.random.split(jax.random.fold_in(part_splits[7], 1), TOKENS // ROWS_DEV)
    routes_turns = jax.random.permutation(jax.random.fold_in(part_splits[7], 3), TOKENS // ROWS_DEV)
    routes = jax.vmap(lambda own, number: shared_out(jax.random.fold_in(part_splits[7], 2), own, number, ROWS_DEV, EXPERTS, TOP, CAP, 2))(routes_keys, routes_turns).reshape((TOKENS, TOP))
    gate_codes = touch_ends(jax.random.randint(part_splits[8], (TOKENS, TOP), 1, 257), jax.random.fold_in(part_splits[8], 1), 1, 256).astype(jnp.int32)
    w_gate = scatter_about(arg_keys[9], (EXPERTS, D, FF), D ** -0.5, 0.15625, ((0, 8), (2, 2)))
    w_up = scatter_about(arg_keys[10], (EXPERTS, D, FF), D ** -0.5, 0.15625, ((0, 8), (2, 2)))
    w_down = scatter_about(arg_keys[11], (EXPERTS, FF, D), FF ** -0.5, 0.15625, ((0, 8), (1, 2)))
    return {"queries": queries, "key_rows": key_rows, "values": values, "sink_logit": sink_logit, "o_weight": o_weight, "residual": residual, "norm_gain": norm_gain, "routes": routes, "gate_codes": gate_codes, "w_gate": w_gate, "w_up": w_up, "w_down": w_down}


def swiglu(gate_val, up_val):
    return (up_val + 1.0) * gate_val * jax.nn.sigmoid(1.702 * gate_val)

def rms_norm(stream, norm_gain):
    widened = stream.astype(jnp.float32)
    spread = lax.optimization_barrier(jnp.mean(widened * widened, axis=-1, keepdims=True))
    return (widened * lax.rsqrt(spread + 1e-05) * norm_gain).astype(jnp.bfloat16)

def window_attention(queries, key_rows, values, sink_logit):
    group_size = HEADS // KV_HEADS
    blocks = TOKENS // TOK_DEV
    kv_width = KV_HEADS * HEAD_DIM
    padded_keys = jnp.concatenate([jnp.zeros((WINDOW, kv_width), key_rows.dtype), key_rows], axis=0)
    padded_values = jnp.concatenate([jnp.zeros((WINDOW, kv_width), values.dtype), values], axis=0)
    sink_vals = sink_logit.astype(jnp.float32).reshape(KV_HEADS, group_size)[:, :, None, None]

    def one_block(block_start):
        block_q = lax.dynamic_slice_in_dim(queries, block_start, TOK_DEV, 0).astype(jnp.float32)
        block_q = block_q.reshape(TOK_DEV, KV_HEADS, group_size, HEAD_DIM)
        block_k = lax.dynamic_slice_in_dim(padded_keys, block_start, TOK_DEV + WINDOW, 0).astype(jnp.float32)
        block_k = block_k.reshape(TOK_DEV + WINDOW, KV_HEADS, HEAD_DIM)
        block_v = lax.dynamic_slice_in_dim(padded_values, block_start, TOK_DEV + WINDOW, 0).astype(jnp.float32)
        block_v = block_v.reshape(TOK_DEV + WINDOW, KV_HEADS, HEAD_DIM)
        scores = jnp.einsum('tgjd,ugd->gjtu', block_q, block_k, precision=lax.Precision.HIGHEST) * HEAD_DIM ** (-0.5)
        query_pos = block_start + jnp.arange(TOK_DEV, dtype=jnp.int32)[:, None]
        key_pos = block_start - WINDOW + jnp.arange(TOK_DEV + WINDOW, dtype=jnp.int32)[None, :]
        allowed = (key_pos <= query_pos) & (key_pos > query_pos - WINDOW) & (key_pos >= 0)
        scores = jnp.where(allowed, scores, -1e+30)
        ceiling = jnp.maximum(lax.optimization_barrier(jnp.max(scores, axis=-1, keepdims=True)), sink_vals)
        raised = jnp.exp(scores - ceiling)
        denominator = lax.optimization_barrier(jnp.sum(raised, axis=-1, keepdims=True)) + jnp.exp(sink_vals - ceiling)
        weights = (raised / denominator).astype(jnp.bfloat16)
        mixed = jnp.einsum('gjtu,ugd->tgjd', weights.astype(jnp.float32), block_v, precision=lax.Precision.HIGHEST)
        return mixed.astype(jnp.bfloat16).reshape(TOK_DEV, HEADS * HEAD_DIM)
    starts = jnp.arange(blocks, dtype=jnp.int32) * TOK_DEV
    return lax.map(one_block, starts).reshape(TOKENS, HEADS * HEAD_DIM)

def mix_experts(normed, routes, gate_codes, w_gate, w_up, w_down):
    sources = TOKENS // ROWS_DEV
    block_ids = routes.reshape(sources, ROWS_DEV * TOP)
    matches = (block_ids[:, :, None] == jnp.arange(EXPERTS, dtype=jnp.int32)[None, None, :]).astype(jnp.int32)
    within = lax.optimization_barrier(jnp.sum((jnp.cumsum(matches, axis=1) - 1) * matches, axis=2))
    column = (jnp.arange(sources, dtype=jnp.int32)[:, None] * CAP + within).reshape(-1)
    pair_ids = block_ids.reshape(-1)
    token_of = jnp.arange(TOKENS * TOP, dtype=jnp.int32) // TOP
    inbox_rows = jnp.zeros((EXPERTS, sources * CAP, D), jnp.bfloat16).at[pair_ids, column].set(normed[token_of])

    def one_expert(operands):
        rows_in, gate_w, up_w, down_w = operands
        gate_val = jnp.dot(rows_in, gate_w, preferred_element_type=jnp.float32)
        up_val = jnp.dot(rows_in, up_w, preferred_element_type=jnp.float32)
        hidden = swiglu(gate_val, up_val).astype(jnp.bfloat16)
        return jnp.dot(hidden, down_w, preferred_element_type=jnp.float32)
    outputs = lax.map(one_expert, (inbox_rows, w_gate, w_up, w_down))
    picked = outputs[pair_ids, column]
    code_vals = gate_codes.astype(jnp.float32)
    shares = code_vals / lax.optimization_barrier(jnp.sum(code_vals, axis=1, keepdims=True))
    mixture = lax.optimization_barrier(jnp.sum(picked.reshape(TOKENS, TOP, D) * shares[:, :, None], axis=1))
    return mixture.astype(jnp.bfloat16)

def reference(queries, key_rows, values, sink_logit, o_weight, residual, norm_gain, routes, gate_codes, w_gate, w_up, w_down):
    heads_out = window_attention(queries, key_rows, values, sink_logit)
    attn_proj = jnp.dot(heads_out, o_weight, preferred_element_type=jnp.float32)
    attended = (residual.astype(jnp.float32) + attn_proj).astype(jnp.bfloat16)
    normed = rms_norm(attended, norm_gain)
    return (attended, mix_experts(normed, routes, gate_codes, w_gate, w_up, w_down))
```

```python
import functools

import jax
import jax.numpy as jnp
from jax import lax
from jax.experimental import pallas as pl
from jax.experimental.pallas import tpu as pltpu
from jax.sharding import PartitionSpec as P

HEAD_DIM = 64
WINDOW = 128
TOP = 4


def shifted(value, axis, steps):
    count = lax.axis_size(axis)
    first, last = (max(0, -steps), min(count, count - steps))
    return lax.ppermute(value, axis, [(source, source + steps) for source in range(first, last)])


def swiglu(gate_val, up_val):
    return (up_val + 1.0) * gate_val * jax.nn.sigmoid(1.702 * gate_val)


def rms_norm(stream, norm_gain):
    widened = stream.astype(jnp.float32)
    spread = jnp.mean(widened * widened, axis=-1, keepdims=True)
    return (widened * lax.rsqrt(spread + 1e-05) * norm_gain).astype(jnp.bfloat16)


def window_attention(queries, key_rows, values, sink_logit):
    row_count = queries.shape[0]
    kv_local = key_rows.shape[1] // HEAD_DIM
    group_size = queries.shape[1] // HEAD_DIM // kv_local
    rim_keys, rim_values = shifted(
        (key_rows[row_count - WINDOW :], values[row_count - WINDOW :]), "seq", 1
    )
    full_keys = jnp.concatenate([rim_keys, key_rows], axis=0).reshape(
        WINDOW + row_count, kv_local, HEAD_DIM
    )
    full_values = jnp.concatenate([rim_values, values], axis=0).reshape(
        WINDOW + row_count, kv_local, HEAD_DIM
    )
    grouped = queries.reshape(row_count, kv_local, group_size, HEAD_DIM)
    scores = jnp.einsum(
        "tgjd,ugd->gjtu", grouped, full_keys, preferred_element_type=jnp.float32
    ) * HEAD_DIM ** (-0.5)
    query_pos = jnp.arange(row_count, dtype=jnp.int32)[:, None] + WINDOW
    key_pos = jnp.arange(WINDOW + row_count, dtype=jnp.int32)[None, :]
    first_key = jnp.where(lax.axis_index("seq") == 0, WINDOW, 0)
    allowed = (key_pos <= query_pos) & (key_pos > query_pos - WINDOW) & (key_pos >= first_key)
    scores = jnp.where(allowed, scores, -1e30)
    sink_vals = sink_logit.reshape(kv_local, group_size)[:, :, None, None]
    ceiling = jnp.maximum(jnp.max(scores, axis=-1, keepdims=True), sink_vals)
    raised = jnp.exp(scores - ceiling)
    denominator = jnp.sum(raised, axis=-1, keepdims=True) + jnp.exp(sink_vals - ceiling)
    weights = (raised / denominator).astype(jnp.bfloat16)
    mixed = jnp.einsum("gjtu,ugd->tgjd", weights, full_values, preferred_element_type=jnp.float32)
    return mixed.astype(jnp.bfloat16).reshape(row_count, kv_local * group_size * HEAD_DIM)


def pack_rows(normed, expert_ids, gate_codes, expert_count, capacity):
    pair_ids = expert_ids.reshape(-1)
    matches = (pair_ids[:, None] == jnp.arange(expert_count, dtype=jnp.int32)[None, :]).astype(
        jnp.float32
    )
    order = jnp.arange(pair_ids.shape[0], dtype=jnp.int32)
    earlier = (order[:, None] > order[None, :]).astype(jnp.bfloat16)
    before = jnp.dot(earlier, matches.astype(jnp.bfloat16), preferred_element_type=jnp.float32)
    within = jnp.sum(before * matches, axis=1).astype(jnp.int32)
    sources = normed[jnp.arange(pair_ids.shape[0], dtype=jnp.int32) // expert_ids.shape[1]]
    outbox = jnp.zeros((expert_count * capacity, normed.shape[1]), normed.dtype)
    outbox = outbox.at[pair_ids * capacity + within].set(sources)
    code_vals = gate_codes.astype(jnp.float32)
    shares = (code_vals / jnp.sum(code_vals, axis=1, keepdims=True)).reshape(-1)
    return (outbox, pair_ids, within, shares)


def expert_apply(arrived, w_gate, w_up, w_down):
    flat_rows = arrived.reshape(-1, arrived.shape[-1])
    gate_val = jnp.dot(flat_rows, w_gate[0], preferred_element_type=jnp.float32)
    up_val = jnp.dot(flat_rows, w_up[0], preferred_element_type=jnp.float32)
    hidden = swiglu(gate_val, up_val).astype(jnp.bfloat16)
    result = jnp.dot(hidden, w_down[0], preferred_element_type=jnp.float32)
    return result.reshape(arrived.shape)


LANES = 128
INNER = 2
PIECES = 3
ITEMS = 2 * PIECES - 1
LAG = 2
CODE_ROWS = 16
MESH = pl.DeviceIdType.MESH


def attend_block(me, block, sink_ref, query_buf, key_buf, value_buf, heads):
    start = block * WINDOW
    lane = lax.broadcasted_iota(jnp.int32, (2 * WINDOW, LANES), 1)
    query_pos = lax.broadcasted_iota(jnp.int32, (WINDOW, 2 * WINDOW), 0) + WINDOW
    key_pos = lax.broadcasted_iota(jnp.int32, (WINDOW, 2 * WINDOW), 1)
    first_key = jnp.where(me == 0, WINDOW, 0) if block == 0 else 0
    allowed = (key_pos <= query_pos) & (key_pos > query_pos - WINDOW) & (key_pos >= first_key)

    def halves(buf, head):
        plain = buf[start : start + 2 * WINDOW, :].astype(jnp.float32)
        turned = pltpu.roll(plain, HEAD_DIM, axis=1)
        low, high = (plain, turned) if head == 0 else (turned, plain)
        return jnp.concatenate(
            [jnp.where(lane < HEAD_DIM, low, 0.0), jnp.where(lane < HEAD_DIM, 0.0, high)], axis=0
        ).astype(jnp.bfloat16)

    pairs = query_buf.shape[1] // LANES
    for head in range(2):
        both_keys = halves(key_buf, head) * jnp.bfloat16(HEAD_DIM ** (-0.5))
        both_values = halves(value_buf, head)
        for pair in range(head * pairs // 2, (head + 1) * pairs // 2):
            columns = slice(pair * LANES, (pair + 1) * LANES)
            scores = lax.dot_general(
                query_buf[start : start + WINDOW, columns], both_keys,
                (((1,), (1,)), ((), ())), preferred_element_type=jnp.float32,
            )
            weights = []
            for half in range(2):
                sink = sink_ref[2 * pair + half]
                part_scores = scores[:, half * 2 * WINDOW : (half + 1) * 2 * WINDOW]
                part_scores = jnp.where(allowed, part_scores, -1e30)
                ceiling = jnp.maximum(jnp.max(part_scores, axis=1, keepdims=True), sink)
                raised = jnp.exp(part_scores - ceiling)
                below = jnp.sum(raised, axis=1, keepdims=True) + jnp.exp(sink - ceiling)
                weights.append((raised * (1.0 / below)).astype(jnp.bfloat16))
            mixed = jnp.dot(
                jnp.concatenate(weights, axis=1), both_values, preferred_element_type=jnp.float32
            )
            heads[start : start + WINDOW, columns] = mixed.astype(jnp.bfloat16)


def layer_kernel(
    sink_ref, gain_ref, routes_ref, codes_ref, query_hbm, key_hbm, value_hbm,
    o_hbm, residual_hbm, gate_hbm, up_hbm, down_hbm, attended_ref, out_ref,
    query_buf, key_buf, value_buf, o_buf, residual_buf, heads, gain_cols, proj_out, proj_in,
    rim_send, rim_recv, proj_send, proj_recv, rows, part, from_core, chain_in, turn_in, cross_in,
    gate_w, up_w, down_w, gate_t, up_t, down_t,
    local_sem, rows_recv, core_send, pair_send, high_send, low_send,
    half_send, half_recv, chain_send, chain_recv, turn_send, turn_recv, cross_send, cross_recv,
):
    me = lax.axis_index("seq")
    core = lax.axis_index("exp")
    other = 1 - core
    count = lax.axis_size("seq")
    outer = count // INNER
    line = me // INNER
    side = me % INNER
    has_low = jnp.minimum(line, 1)
    has_high = jnp.minimum(outer - 1 - line, 1)
    to_core = {"exp": other}
    to_pair = {"seq": line * INNER + 1 - side}
    to_high = {"seq": jnp.minimum(line + 1, outer - 1) * INNER + side}
    to_low = {"seq": jnp.maximum(line - 1, 0) * INNER + side}
    feature_dim = attended_ref.shape[0]
    piece = feature_dim // PIECES
    later = tuple(range(1, PIECES))

    def chip_of(at, at_side):
        return at * INNER + at_side

    def send(src, dst, send_sem, recv_sem, where):
        return pltpu.make_async_remote_copy(
            src_ref=src, dst_ref=dst, send_sem=send_sem, recv_sem=recv_sem,
            device_id=where, device_id_type=MESH,
        )

    def row_copy(chip, of_core, send_sem, where):
        slot = rows.at[chip, of_core]
        return send(slot, slot, send_sem, rows_recv.at[chip, of_core], where)

    block_rows = proj_in.shape[1]
    row_count = query_buf.shape[0]
    has_prev = jnp.minimum(me, 1)
    has_next = jnp.minimum(count - 1 - me, 1)
    to_prev = {"seq": jnp.maximum(me - 1, 0)}
    to_next = {"seq": jnp.minimum(me + 1, count - 1)}
    own_rows = pl.ds(pl.multiple_of(core * block_rows, LANES), block_rows)
    other_rows = pl.ds(pl.multiple_of(other * block_rows, LANES), block_rows)
    inside = pl.ds(WINDOW, row_count)
    pieces = (
        (key_hbm, key_buf.at[inside]),
        (value_hbm, value_buf.at[inside]),
        (query_hbm, query_buf),
        (o_hbm, o_buf),
        (residual_hbm.at[:, own_rows], residual_buf),
        (gate_hbm.at[0], gate_w),
        (up_hbm.at[0], up_w),
        (down_hbm.at[0], down_w),
    )
    copies = [
        pltpu.make_async_copy(src, dst, local_sem.at[index])
        for index, (src, dst) in enumerate(pieces)
    ]
    for copy in copies:
        copy.start()
    barrier = pltpu.get_barrier_semaphore()
    pl.semaphore_signal(barrier, inc=1, device_id=to_core, device_id_type=MESH)
    pl.semaphore_signal(barrier, inc=1, device_id=to_pair, device_id_type=MESH)

    @pl.when(has_low == 1)
    def _():
        pl.semaphore_signal(barrier, inc=1, device_id=to_low, device_id_type=MESH)

    @pl.when(has_high == 1)
    def _():
        pl.semaphore_signal(barrier, inc=1, device_id=to_high, device_id_type=MESH)

    @pl.when(has_prev == 1)
    def _():
        pl.semaphore_signal(barrier, inc=1, device_id=to_prev, device_id_type=MESH)

    @pl.when(has_next == 1)
    def _():
        pl.semaphore_signal(barrier, inc=1, device_id=to_next, device_id_type=MESH)

    gain_cols[...] = jnp.broadcast_to(
        gain_ref[...].reshape(1, -1), (block_rows, feature_dim)
    ).T
    pl.semaphore_wait(barrier, 2 + has_low + has_high + has_prev + has_next)
    for copy in copies[:2]:
        copy.wait()

    def rim_copy(index, buf):
        return send(
            buf.at[pl.ds(row_count, WINDOW)], buf.at[pl.ds(0, WINDOW)],
            rim_send.at[index], rim_recv.at[index], to_next,
        )

    rims = (rim_copy(0, key_buf), rim_copy(1, value_buf))

    @pl.when(has_next == 1)
    def _():
        for copy in rims:
            copy.start()

    copies[2].wait()
    attend_block(me, 1, sink_ref, query_buf, key_buf, value_buf, heads)

    @pl.when(has_prev == 1)
    def _():
        for copy in rims:
            copy.wait_recv()

    @pl.when(has_prev == 0)
    def _():
        key_buf[:WINDOW] = jnp.zeros((WINDOW, key_buf.shape[1]), key_buf.dtype)
        value_buf[:WINDOW] = jnp.zeros((WINDOW, value_buf.shape[1]), value_buf.dtype)

    attend_block(me, 0, sink_ref, query_buf, key_buf, value_buf, heads)
    for copy in copies[3:5]:
        copy.wait()

    proj_copy = send(proj_out, proj_in, proj_send.at[0], proj_recv.at[0], to_core)

    def project(which):
        return lax.dot_general(
            o_buf[...], heads[which, :], (((1,), (1,)), ((), ())),
            preferred_element_type=jnp.float32,
        )

    proj_out[...] = project(other_rows).astype(jnp.bfloat16)
    proj_copy.start()
    stream = residual_buf[...].astype(jnp.float32) + project(own_rows)
    own_routes = routes_ref[:, own_rows]
    own_codes = codes_ref[:, own_rows].astype(jnp.float32)
    code_rows = rows.shape[2] - feature_dim
    expert = lax.broadcasted_iota(jnp.int32, (code_rows, block_rows), 0)
    spread = jnp.zeros((code_rows, block_rows), jnp.float32)
    for choice in range(TOP):
        named = expert == own_routes[choice : choice + 1, :]
        spread = jnp.where(named, own_codes[choice : choice + 1, :], spread)
    rows[me, core, feature_dim:, :] = spread.astype(jnp.bfloat16)
    proj_copy.wait_recv()
    attended = (stream + proj_in[...].astype(jnp.float32)).astype(jnp.bfloat16)
    attended_ref[...] = attended
    widened = attended.astype(jnp.float32)
    mean = jnp.sum(widened * widened, axis=0, keepdims=True) / feature_dim
    rows[me, core, :feature_dim, :] = (
        widened * lax.rsqrt(mean + 1e-05) * gain_cols[...]
    ).astype(jnp.bfloat16)

    def place(dist, sign):
        at = line + sign * dist
        first = 0 if sign > 0 else 1
        return at, (at >= 0) & (at < outer) & (dist >= first) & (dist < outer)

    def relay_line(dist, sign):
        at, valid = place(dist, sign)

        @pl.when(valid)
        def _():
            chip = chip_of(at, side)

            @pl.when(dist > 0)
            def _():
                row_copy(chip, core, core_send.at[chip], to_core).wait_recv()

            @pl.when((at <= line) & (has_high == 1))
            def _():
                row_copy(chip, core, high_send.at[at], to_high).start()

            @pl.when((at >= line) & (has_low == 1))
            def _():
                row_copy(chip, core, low_send.at[at], to_low).start()

            row_copy(chip, core, pair_send.at[at], to_pair).start()
            row_copy(chip, core, core_send.at[chip], to_core).start()

    def relay_pair(dist, sign):
        at, valid = place(dist, sign)

        @pl.when(valid)
        def _():
            chip = chip_of(at, 1 - side)
            row_copy(chip, core, core_send.at[chip], to_core).wait_recv()
            row_copy(chip, core, core_send.at[chip], to_core).start()

    def half_copy(chip):
        return send(
            part.at[chip, other], from_core.at[chip], half_send.at[chip], half_recv.at[chip], to_core
        )

    def compute(chip):
        codes = jnp.concatenate(
            [rows[chip, 0, feature_dim:, :], rows[chip, 1, feature_dim:, :]], axis=1
        ).astype(jnp.float32)
        expert = lax.broadcasted_iota(jnp.int32, codes.shape, 0)
        total = jnp.sum(codes, axis=0, keepdims=True)
        mine = jnp.sum(jnp.where(expert == me, codes, 0.0), axis=0, keepdims=True)
        normed = jnp.concatenate(
            [rows[chip, 0, :feature_dim, :], rows[chip, 1, :feature_dim, :]], axis=1
        )
        gate_val = jnp.dot(gate_t[...], normed, preferred_element_type=jnp.float32)
        up_val = jnp.dot(up_t[...], normed, preferred_element_type=jnp.float32)
        hidden = swiglu(gate_val, up_val).astype(jnp.bfloat16)
        result = jnp.dot(down_t[...], hidden, preferred_element_type=jnp.float32)
        result = (result * (mine / total)).astype(jnp.bfloat16)
        part[chip, 0] = result[:, :block_rows]
        part[chip, 1] = result[:, block_rows:]
        half_copy(chip).start()

    def widen(value):
        return value.astype(jnp.float32)

    def span(index):
        return pl.ds(pl.multiple_of(index * piece, 16), piece)

    def own_sum(chip, index):
        return widen(part[chip, core, span(index), :]) + widen(from_core[chip, span(index), :])

    def turn_copy(at):
        return send(
            part.at[chip_of(at, 1 - side), core, span(0)], turn_in.at[at],
            turn_send.at[at], turn_recv.at[at], to_pair,
        )

    def chain_copy(at, cross, index, sign):
        chip = chip_of(at, side + cross * (1 - 2 * side))
        way = 1 if sign > 0 else 0
        return send(
            part.at[chip, core, span(index)], chain_in.at[way, cross, at, span(index)],
            chain_send.at[cross, at, index], chain_recv.at[way, cross, at, index],
            to_high if sign > 0 else to_low,
        )

    def cross_copy(index):
        return send(
            part.at[chip_of(line, 1 - side), core, span(index)], cross_in.at[span(index)],
            cross_send.at[index], cross_recv.at[index], to_pair,
        )

    def turn(dist, sign):
        at, valid = place(dist, sign)

        @pl.when(valid)
        def _():
            chip = chip_of(at, 1 - side)
            half_copy(chip).wait_recv()
            part[chip, core, span(0), :] = own_sum(chip, 0).astype(jnp.bfloat16)
            turn_copy(at).start()

    def chain(step, sign):
        hops = line if sign > 0 else outer - 1 - line
        place_in = step - LAG * hops
        turn_at = 2 * len(later)
        group, slot = (place_in + ITEMS) // ITEMS, (place_in + ITEMS) % ITEMS
        own_group = slot < len(later)
        cross = jnp.where((slot >= len(later)) & (slot < turn_at), 1, 0)
        reach = jnp.where(own_group, group, group - 1)
        index = jnp.where(slot == turn_at, 0, 1 + slot % len(later))
        at = reach if sign > 0 else outer - 1 - reach
        ahead = (at > line) if sign > 0 else (at < line)
        way = 1 if sign > 0 else 0

        @pl.when((place_in >= 0) & (reach >= 1) & (reach < outer) & ahead)
        def _():
            chip = chip_of(at, side + cross * (1 - 2 * side))

            @pl.when(slot == 0)
            def _():
                half_copy(chip).wait_recv()

            @pl.when(slot == turn_at)
            def _():
                turn_copy(at).wait_recv()
                part[chip, core, span(0), :] = (
                    widen(part[chip, core, span(0), :]) + widen(turn_in[at])
                ).astype(jnp.bfloat16)

            @pl.when(hops > 0)
            def _():
                chain_copy(at, cross, index, sign).wait_recv()
                part[chip, core, span(index), :] = (
                    own_sum(chip, index) + widen(chain_in[way, cross, at, span(index), :])
                ).astype(jnp.bfloat16)

            @pl.when(hops == 0)
            def _():
                part[chip, core, span(index), :] = own_sum(chip, index).astype(jnp.bfloat16)

            chain_copy(at, cross, index, sign).start()

    def chain_both(step, carry):
        chain(step, 1)
        chain(step, -1)
        return carry

    def gather_step(dist, carry):
        relay_line(dist, -1)
        relay_line(dist, 1)
        relay_pair(dist - 1, -1)
        relay_pair(dist - 1, 1)

        @pl.when(dist == 0)
        def _():
            for copy in copies[5:]:
                copy.wait()
            gate_t[...] = gate_w[...].T
            up_t[...] = up_w[...].T
            down_t[...] = down_w[...].T

        def one(index, inner_carry):
            lag = index // 2
            sign = 2 * (index % 2) - 1
            far = dist - lag
            at = line + sign * far
            first = 1 - index % 2
            valid = (at >= 0) & (at < outer) & (far >= first) & (far < outer)

            @pl.when(valid)
            def _():
                chip = chip_of(at, side + lag * (1 - 2 * side))
                row_copy(chip, other, core_send.at[chip], to_core).wait_recv()
                compute(chip)

            return inner_carry

        lax.fori_loop(0, 4, one, carry)
        turn(dist - 1, -1)
        turn(dist - 1, 1)

        @pl.when(dist > 0)
        def _():
            lax.fori_loop(ITEMS * (dist - 1), ITEMS * dist, chain_both, 0)

        return carry

    lax.fori_loop(0, outer + 1, gather_step, 0)
    lax.fori_loop(ITEMS * outer, ITEMS * outer + LAG * (outer - 1), chain_both, 0)

    def gathered(cross, index, store):
        chip = chip_of(line, 1 - side if cross else side)
        total = own_sum(chip, index)
        low = chain_copy(line, cross, index, 1)
        high = chain_copy(line, cross, index, -1)

        @pl.when(has_low == 1)
        def _():
            low.wait_recv()

        @pl.when(has_high == 1)
        def _():
            high.wait_recv()

        def arrived(way):
            return widen(chain_in[way, cross, line, span(index), :])

        @pl.when((has_low == 1) & (has_high == 1))
        def _():
            store(total + arrived(1) + arrived(0))

        @pl.when((has_low == 1) & (has_high == 0))
        def _():
            store(total + arrived(1))

        @pl.when((has_low == 0) & (has_high == 1))
        def _():
            store(total + arrived(0))

        @pl.when((has_low == 0) & (has_high == 0))
        def _():
            store(total)

    for index in later:
        def keep(total, index=index):
            part[chip_of(line, 1 - side), core, span(index), :] = total.astype(jnp.bfloat16)

        gathered(1, index, keep)
        cross_copy(index).start()

    half_copy(me).wait_recv()
    turn_copy(line).wait_recv()

    def finish_first(total):
        out_ref[span(0), :] = (total + widen(turn_in[line])).astype(jnp.bfloat16)

    gathered(0, 0, finish_first)
    for index in later:
        def finish(total, index=index):
            cross_copy(index).wait_recv()
            out_ref[span(index), :] = (
                total + widen(cross_in[span(index), :])
            ).astype(jnp.bfloat16)

        gathered(0, index, finish)

    def drain(at, carry):
        chip = chip_of(at, side)

        @pl.when((at <= line) & (has_high == 1))
        def _():
            row_copy(chip, core, high_send.at[at], to_high).wait_send()

        @pl.when((at >= line) & (has_low == 1))
        def _():
            row_copy(chip, core, low_send.at[at], to_low).wait_send()

        row_copy(chip, core, pair_send.at[at], to_pair).wait_send()
        row_copy(chip, core, core_send.at[chip], to_core).wait_send()
        half_copy(chip).wait_send()
        across = chip_of(at, 1 - side)
        row_copy(across, core, core_send.at[across], to_core).wait_send()
        half_copy(across).wait_send()
        turn_copy(at).wait_send()

        @pl.when(at > line)
        def _():
            for index in range(PIECES):
                chain_copy(at, 0, index, 1).wait_send()
            for index in later:
                chain_copy(at, 1, index, 1).wait_send()

        @pl.when(at < line)
        def _():
            for index in range(PIECES):
                chain_copy(at, 0, index, -1).wait_send()
            for index in later:
                chain_copy(at, 1, index, -1).wait_send()

        return carry

    lax.fori_loop(0, outer, drain, 0)
    for index in later:
        cross_copy(index).wait_send()
    proj_copy.wait_send()

    @pl.when(has_next == 1)
    def _():
        for copy in rims:
            copy.wait_send()


def whole_layer(
    queries, key_rows, values, sink_logit, o_weight, residual, norm_gain, routes, gate_codes,
    w_gate, w_up, w_down,
):
    row_count, feature_dim = residual.shape
    block_rows = row_count // 2
    chips = lax.axis_size("seq")
    outer = chips // INNER
    hidden_dim = w_gate.shape[2]
    turned = (feature_dim, block_rows)
    coded = (feature_dim + CODE_ROWS, block_rows)
    dma = pltpu.SemaphoreType.DMA
    vmem = pl.BlockSpec(memory_space=pltpu.VMEM)
    half = jnp.bfloat16
    attended, mixture = pl.pallas_call(
        layer_kernel,
        out_shape=(jax.ShapeDtypeStruct(turned, half), jax.ShapeDtypeStruct(turned, half)),
        in_specs=[pl.BlockSpec(memory_space=pltpu.SMEM), vmem, vmem, vmem]
        + [pl.BlockSpec(memory_space=pl.ANY)] * 8,
        out_specs=(vmem, vmem),
        scratch_shapes=[
            pltpu.VMEM(queries.shape, half),
            pltpu.VMEM((WINDOW + row_count, key_rows.shape[1]), half),
            pltpu.VMEM((WINDOW + row_count, values.shape[1]), half),
            pltpu.VMEM(o_weight.shape[::-1], half),
            pltpu.VMEM(turned, half),
            pltpu.VMEM(queries.shape, half),
            pltpu.VMEM(turned, jnp.float32),
            pltpu.VMEM(turned, half),
            pltpu.VMEM(turned, half),
            dma((2,)),
            dma((2,)),
            dma((1,)),
            dma((1,)),
            pltpu.VMEM((chips, 2) + coded, half),
            pltpu.VMEM((chips, 2) + turned, half),
            pltpu.VMEM((chips,) + turned, half),
            pltpu.VMEM((2, 2, outer) + turned, half),
            pltpu.VMEM((outer, feature_dim // PIECES, block_rows), half),
            pltpu.VMEM(turned, half),
            pltpu.VMEM((feature_dim, hidden_dim), half),
            pltpu.VMEM((feature_dim, hidden_dim), half),
            pltpu.VMEM((hidden_dim, feature_dim), half),
            pltpu.VMEM((hidden_dim, feature_dim), half),
            pltpu.VMEM((hidden_dim, feature_dim), half),
            pltpu.VMEM((feature_dim, hidden_dim), half),
            dma((8,)),
            dma((chips, 2)),
            dma((chips,)),
            dma((outer,)),
            dma((outer,)),
            dma((outer,)),
            dma((chips,)),
            dma((chips,)),
            dma((2, outer, PIECES)),
            dma((2, 2, outer, PIECES)),
            dma((outer,)),
            dma((outer,)),
            dma((PIECES,)),
            dma((PIECES,)),
        ],
        compiler_params=pltpu.CompilerParams(
            collective_id=1, has_side_effects=True, vmem_limit_bytes=60 << 20
        ),
    )(
        sink_logit, norm_gain, routes.T, gate_codes.T, queries, key_rows, values,
        o_weight.T, residual.T, w_gate, w_up, w_down,
    )
    return (attended.T, mixture.T)


def fits_kernel(queries, key_rows, residual, w_gate):
    chips = lax.axis_size("seq")
    return (
        lax.axis_size("exp") == 2
        and chips % INNER == 0
        and chips <= CODE_ROWS
        and residual.shape[1] % (16 * PIECES) == 0
        and w_gate.shape[0] == 1
        and residual.shape[0] == 2 * WINDOW
        and 2 * TOP >= chips
        and key_rows.shape[1] == LANES
        and queries.shape[1] % (2 * LANES) == 0
    )


def local(
    queries,
    key_rows,
    values,
    sink_logit,
    o_weight,
    residual,
    norm_gain,
    routes,
    gate_codes,
    w_gate,
    w_up,
    w_down,
):
    if fits_kernel(queries, key_rows, residual, w_gate):
        return whole_layer(
            queries, key_rows, values, sink_logit, o_weight, residual, norm_gain, routes,
            gate_codes, w_gate, w_up, w_down,
        )
    heads_out = window_attention(queries, key_rows, values, sink_logit)
    proj_terms = jnp.dot(heads_out, o_weight, preferred_element_type=jnp.float32)
    owners = lax.axis_size("exp")
    owner_pos = lax.axis_index("exp")
    block_rows = residual.shape[0] // owners
    expert_count = w_gate.shape[0] * lax.axis_size("seq")
    capacity = max(2, 2 * block_rows * TOP // expert_count)
    feature_dim = residual.shape[1]
    own_stream = lax.dynamic_slice_in_dim(residual, owner_pos * block_rows, block_rows, 0)
    own_routes = lax.dynamic_slice_in_dim(routes, owner_pos * block_rows, block_rows, 0)
    own_codes = lax.dynamic_slice_in_dim(gate_codes, owner_pos * block_rows, block_rows, 0)
    own_terms = lax.psum_scatter(proj_terms, "exp", scatter_dimension=0, tiled=True)
    attended = (own_stream.astype(jnp.float32) + own_terms).astype(jnp.bfloat16)
    normed = rms_norm(attended, norm_gain)
    outbox, pair_ids, within, shares = pack_rows(
        normed, own_routes, own_codes, expert_count, capacity
    )
    partial_value = expert_apply(
        lax.all_gather(
            lax.all_to_all(
                outbox.reshape(expert_count, capacity, feature_dim),
                "seq",
                split_axis=0,
                concat_axis=0,
                tiled=True,
            ),
            "exp",
            axis=0,
            tiled=True,
        ),
        w_gate,
        w_up,
        w_down,
    )
    whole = lax.psum_scatter(
        partial_value.astype(jnp.bfloat16), "exp", scatter_dimension=0, tiled=True
    ).astype(jnp.float32)
    returned = lax.all_to_all(
        whole.astype(jnp.bfloat16), "seq", split_axis=0, concat_axis=0, tiled=True
    ).astype(whole.dtype)
    picked = returned[pair_ids, within]
    mixture = jnp.sum((picked * shares[:, None]).reshape(-1, TOP, feature_dim), axis=1)
    return (attended, mixture.astype(jnp.bfloat16))


def solution(mesh):
    placed = (
        P(("groups", "seq"), "exp"),
        P(("groups", "seq"), "exp"),
        P(("groups", "seq"), "exp"),
        P("exp"),
        P("exp", None),
        P(("groups", "seq"), None),
        P(),
        P(("groups", "seq"), None),
        P(("groups", "seq"), None),
        P("seq", None, "exp"),
        P("seq", None, "exp"),
        P("seq", "exp", None),
    )
    return jax.shard_map(
        local,
        mesh=mesh,
        in_specs=placed,
        out_specs=(P(("groups", "seq", "exp"), None), P(("groups", "seq", "exp"), None)),
        check_vma=False,
    )
```

```python
import functools

import jax
import jax.numpy as jnp
from jax import lax
from jax.experimental import pallas as pl
from jax.experimental.pallas import tpu as pltpu
from jax.sharding import PartitionSpec as P

HEAD_DIM = 64
WINDOW = 128
TOP = 4


def shifted(value, axis, steps):
    count = lax.axis_size(axis)
    first, last = (max(0, -steps), min(count, count - steps))
    return lax.ppermute(value, axis, [(source, source + steps) for source in range(first, last)])


def swiglu(gate_val, up_val):
    return (up_val + 1.0) * gate_val * jax.nn.sigmoid(1.702 * gate_val)


def rms_norm(stream, norm_gain):
    widened = stream.astype(jnp.float32)
    spread = jnp.mean(widened * widened, axis=-1, keepdims=True)
    return (widened * lax.rsqrt(spread + 1e-05) * norm_gain).astype(jnp.bfloat16)


def window_attention(queries, key_rows, values, sink_logit):
    row_count = queries.shape[0]
    kv_local = key_rows.shape[1] // HEAD_DIM
    group_size = queries.shape[1] // HEAD_DIM // kv_local
    rim_keys, rim_values = shifted(
        (key_rows[row_count - WINDOW :], values[row_count - WINDOW :]), "seq", 1
    )
    full_keys = jnp.concatenate([rim_keys, key_rows], axis=0).reshape(
        WINDOW + row_count, kv_local, HEAD_DIM
    )
    full_values = jnp.concatenate([rim_values, values], axis=0).reshape(
        WINDOW + row_count, kv_local, HEAD_DIM
    )
    grouped = queries.reshape(row_count, kv_local, group_size, HEAD_DIM)
    scores = jnp.einsum(
        "tgjd,ugd->gjtu", grouped, full_keys, preferred_element_type=jnp.float32
    ) * HEAD_DIM ** (-0.5)
    query_pos = jnp.arange(row_count, dtype=jnp.int32)[:, None] + WINDOW
    key_pos = jnp.arange(WINDOW + row_count, dtype=jnp.int32)[None, :]
    first_key = jnp.where(lax.axis_index("seq") == 0, WINDOW, 0)
    allowed = (key_pos <= query_pos) & (key_pos > query_pos - WINDOW) & (key_pos >= first_key)
    scores = jnp.where(allowed, scores, -1e30)
    sink_vals = sink_logit.reshape(kv_local, group_size)[:, :, None, None]
    ceiling = jnp.maximum(jnp.max(scores, axis=-1, keepdims=True), sink_vals)
    raised = jnp.exp(scores - ceiling)
    denominator = jnp.sum(raised, axis=-1, keepdims=True) + jnp.exp(sink_vals - ceiling)
    weights = (raised / denominator).astype(jnp.bfloat16)
    mixed = jnp.einsum("gjtu,ugd->tgjd", weights, full_values, preferred_element_type=jnp.float32)
    return mixed.astype(jnp.bfloat16).reshape(row_count, kv_local * group_size * HEAD_DIM)


def pack_rows(normed, expert_ids, gate_codes, expert_count, capacity):
    pair_ids = expert_ids.reshape(-1)
    matches = (pair_ids[:, None] == jnp.arange(expert_count, dtype=jnp.int32)[None, :]).astype(
        jnp.float32
    )
    order = jnp.arange(pair_ids.shape[0], dtype=jnp.int32)
    earlier = (order[:, None] > order[None, :]).astype(jnp.bfloat16)
    before = jnp.dot(earlier, matches.astype(jnp.bfloat16), preferred_element_type=jnp.float32)
    within = jnp.sum(before * matches, axis=1).astype(jnp.int32)
    sources = normed[jnp.arange(pair_ids.shape[0], dtype=jnp.int32) // expert_ids.shape[1]]
    outbox = jnp.zeros((expert_count * capacity, normed.shape[1]), normed.dtype)
    outbox = outbox.at[pair_ids * capacity + within].set(sources)
    code_vals = gate_codes.astype(jnp.float32)
    shares = (code_vals / jnp.sum(code_vals, axis=1, keepdims=True)).reshape(-1)
    return (outbox, pair_ids, within, shares)


def expert_apply(arrived, w_gate, w_up, w_down):
    flat_rows = arrived.reshape(-1, arrived.shape[-1])
    gate_val = jnp.dot(flat_rows, w_gate[0], preferred_element_type=jnp.float32)
    up_val = jnp.dot(flat_rows, w_up[0], preferred_element_type=jnp.float32)
    hidden = swiglu(gate_val, up_val).astype(jnp.bfloat16)
    result = jnp.dot(hidden, w_down[0], preferred_element_type=jnp.float32)
    return result.reshape(arrived.shape)


LANES = 128
INNER = 2
CODE_ROWS = 16
PROJ_CUTS = 3
RELAY, AWAIT, APPLY, TURN, CHAIN, CROSS, FINISH = range(7)
ROW_TURNS = (0, 0, 1)
PIECE_TURNS = (1, 1, 0, 0, 0)
ORDERS = (
    (
        (RELAY, 0, 0, 0), (RELAY, 0, 0, 1), (RELAY, 0, 0, 2), (APPLY, 0, 0), (RELAY, 1, 0, 2),
        (AWAIT, 0, 0), (RELAY, 1, 0, 0), (RELAY, 1, 0, 1), (APPLY, 1, 0), (RELAY, 1, 1, 2),
        (AWAIT, 1, 1), (AWAIT, 1, 0), (CHAIN, 1, 0, 4, 1), (RELAY, 0, 1, 2), (RELAY, 2, 0, 0),
        (AWAIT, 0, 1), (APPLY, 1, 1), (APPLY, 0, 1), (RELAY, 2, 0, 2), (RELAY, 2, 0, 1),
        (CHAIN, 1, 1, 3, 1), (CHAIN, 1, 0, 3, 1), (AWAIT, 2, 0), (CHAIN, 1, 1, 2, 1), (APPLY, 2, 0),
        (RELAY, 2, 1, 2), (AWAIT, 2, 1), (RELAY, 3, 0, 1), (CHAIN, 2, 0, 4, 1), (CHAIN, 2, 0, 3, 1),
        (APPLY, 2, 1), (RELAY, 3, 0, 0), (CHAIN, 2, 0, 2, 1), (RELAY, 3, 0, 2), (CHAIN, 2, 1, 4, 1),
        (CHAIN, 2, 1, 2, 1), (APPLY, 3, 0), (CHAIN, 2, 1, 3, 1), (CHAIN, 3, 0, 3, 1), (RELAY, 3, 1, 2),
        (AWAIT, 3, 0), (CHAIN, 3, 0, 4, 1), (AWAIT, 3, 1), (TURN, 1, 1), (CHAIN, 3, 0, 2, 1),
        (TURN, 2, 0), (APPLY, 3, 1), (CHAIN, 1, 1, 4, 1), (TURN, 3, 1), (CHAIN, 3, 1, 3, 1),
        (CHAIN, 3, 1, 2, 1), (TURN, 3, 0), (CHAIN, 3, 1, 4, 1), (TURN, 2, 1), (CHAIN, 3, 0, 1, 1),
        (CHAIN, 3, 0, 0, 1), (TURN, 1, 0), (CHAIN, 2, 0, 1, 1), (TURN, 0, 0), (CHAIN, 1, 0, 1, 1),
        (TURN, 0, 1), (CHAIN, 2, 0, 0, 1), (CHAIN, 1, 0, 2, 1), (CROSS, 3), (CROSS, 2),
        (CHAIN, 1, 0, 0, 1), (CROSS, 4), (FINISH, 1), (FINISH, 2), (FINISH, 3), (FINISH, 0),
        (FINISH, 4),
    ),
    (
        (RELAY, 1, 0, 2), (RELAY, 1, 0, 0), (RELAY, 1, 0, 1), (RELAY, 1, 1, 2), (RELAY, 2, 0, 0),
        (RELAY, 0, 0, 1), (RELAY, 0, 0, 0), (RELAY, 2, 0, 1), (AWAIT, 1, 0), (RELAY, 2, 0, 2),
        (RELAY, 3, 0, 1), (RELAY, 0, 0, 2), (APPLY, 2, 0), (RELAY, 2, 1, 2), (AWAIT, 1, 1),
        (APPLY, 1, 0), (AWAIT, 2, 0), (RELAY, 3, 0, 0), (AWAIT, 2, 1), (RELAY, 0, 1, 2),
        (RELAY, 3, 0, 2), (AWAIT, 0, 1), (APPLY, 2, 1), (APPLY, 3, 0), (AWAIT, 0, 0), (RELAY, 3, 1, 2),
        (AWAIT, 3, 1), (APPLY, 0, 1), (AWAIT, 3, 0), (CHAIN, 2, 0, 2, 1), (CHAIN, 2, 0, 4, 1),
        (APPLY, 3, 1), (CHAIN, 2, 1, 4, 1), (CHAIN, 2, 1, 2, 1), (TURN, 2, 0), (APPLY, 0, 0),
        (TURN, 3, 0), (CHAIN, 2, 1, 3, 1), (TURN, 3, 1), (CHAIN, 3, 0, 3, 1), (TURN, 0, 0),
        (CHAIN, 3, 0, 4, 1), (APPLY, 1, 1), (TURN, 2, 1), (CHAIN, 3, 0, 2, 1), (CHAIN, 0, 0, 3, -1),
        (TURN, 1, 0), (CHAIN, 3, 1, 3, 1), (TURN, 0, 1), (CHAIN, 0, 0, 4, -1), (CHAIN, 3, 1, 2, 1),
        (TURN, 1, 1), (CHAIN, 0, 0, 2, -1), (CROSS, 4), (CHAIN, 3, 1, 4, 1), (CHAIN, 0, 1, 3, -1),
        (CROSS, 3), (CHAIN, 3, 0, 1, 1), (CHAIN, 0, 1, 2, -1), (CHAIN, 3, 0, 0, 1),
        (CHAIN, 0, 1, 4, -1), (CHAIN, 2, 0, 3, 1), (CHAIN, 0, 0, 1, -1), (CHAIN, 2, 0, 1, 1),
        (CROSS, 2), (FINISH, 4), (CHAIN, 0, 0, 0, -1), (CHAIN, 2, 0, 0, 1), (FINISH, 1), (FINISH, 2),
        (FINISH, 3), (FINISH, 0),
    ),
)


def cuts_of(extent, parts):
    edges = [extent // 16 * part // parts * 16 for part in range(parts)] + [extent]
    return [(first, last - first) for first, last in zip(edges, edges[1:])]
MESH = pl.DeviceIdType.MESH


def attend_block(me, block, sink_ref, query_buf, key_buf, value_buf, heads):
    start = block * WINDOW
    lane = lax.broadcasted_iota(jnp.int32, (2 * WINDOW, LANES), 1)
    query_pos = lax.broadcasted_iota(jnp.int32, (WINDOW, WINDOW), 0)
    key_pos = lax.broadcasted_iota(jnp.int32, (WINDOW, WINDOW), 1)
    recent = key_pos <= query_pos
    opening = (me == 0) & (block == 0)

    def halves(buf, head):
        plain = buf[start : start + 2 * WINDOW, :].astype(jnp.float32)
        turned = pltpu.roll(plain, HEAD_DIM, axis=1)
        low, high = (plain, turned) if head == 0 else (turned, plain)
        return jnp.concatenate(
            [jnp.where(lane < HEAD_DIM, low, 0.0), jnp.where(lane < HEAD_DIM, 0.0, high)], axis=0
        ).astype(jnp.bfloat16)

    pairs = query_buf.shape[1] // LANES
    for head in range(2):
        both_keys = halves(key_buf, head) * jnp.bfloat16(HEAD_DIM ** (-0.5))
        both_values = halves(value_buf, head)
        for pair in range(head * pairs // 2, (head + 1) * pairs // 2):
            columns = slice(pair * LANES, (pair + 1) * LANES)
            scores = lax.dot_general(
                query_buf[start : start + WINDOW, columns], both_keys,
                (((1,), (1,)), ((), ())), preferred_element_type=jnp.float32,
            )
            weights = []
            for half in range(2):
                sink = sink_ref[2 * pair + half]
                first = 2 * half * WINDOW
                earlier = scores[:, first : first + WINDOW]
                if block == 0:
                    earlier = jnp.where(opening, -1e30, earlier)
                seen = jnp.where(recent, scores[:, first + WINDOW : first + 2 * WINDOW], earlier)
                ceiling = jnp.maximum(jnp.max(seen, axis=1, keepdims=True), sink)
                raised = jnp.exp(seen - ceiling)
                below = jnp.sum(raised, axis=1, keepdims=True) + jnp.exp(sink - ceiling)
                shares = raised * (1.0 / below)
                weights.append(jnp.where(recent, 0.0, shares).astype(jnp.bfloat16))
                weights.append(jnp.where(recent, shares, 0.0).astype(jnp.bfloat16))
            mixed = jnp.dot(
                jnp.concatenate(weights, axis=1), both_values, preferred_element_type=jnp.float32
            )
            heads[start : start + WINDOW, columns] = mixed.astype(jnp.bfloat16)


def layer_kernel(
    sink_ref, gain_ref, routes_ref, codes_ref, query_hbm, key_hbm, value_hbm,
    o_hbm, residual_hbm, gate_hbm, up_hbm, down_hbm, attended_ref, out_ref,
    query_buf, key_buf, value_buf, o_buf, residual_buf, heads, gain_cols, stream, proj_out, proj_in,
    rim_send, rim_recv, proj_send, proj_recv, rows, part, from_core, chain_in, turn_in, cross_in,
    gate_w, up_w, down_w, gate_t, up_t, down_t,
    local_sem, row_recv, others_recv, row_send, half_send, half_recv, chain_send, chain_recv,
    turn_send, turn_recv, cross_send, cross_recv,
):
    me = lax.axis_index("seq")
    core = lax.axis_index("exp")
    other = 1 - core
    count = lax.axis_size("seq")
    outer = count // INNER
    line = me // INNER
    side = me % INNER
    has_low = jnp.minimum(line, 1)
    has_high = jnp.minimum(outer - 1 - line, 1)
    to_core = {"exp": other}
    to_pair = {"seq": line * INNER + 1 - side}
    to_high = {"seq": jnp.minimum(line + 1, outer - 1) * INNER + side}
    to_low = {"seq": jnp.maximum(line - 1, 0) * INNER + side}
    feature_dim = attended_ref.shape[0]
    flip = 2 * line // outer
    step = 1 - 2 * flip
    base = flip * (outer - 1)
    place = base + step * line
    to_ahead = {"seq": jnp.clip(line + step, 0, outer - 1) * INNER + side}
    to_back = {"seq": jnp.clip(line - step, 0, outer - 1) * INNER + side}
    row_cuts = cuts_of(rows.shape[2], len(ROW_TURNS))
    piece_cuts = cuts_of(feature_dim, len(PIECE_TURNS))
    turned_pieces = [index for index, flag in enumerate(PIECE_TURNS) if flag]
    plain_pieces = [index for index, flag in enumerate(PIECE_TURNS) if not flag]

    def chip_of(at, at_side):
        return at * INNER + at_side

    def send(src, dst, send_sem, recv_sem, where):
        return pltpu.make_async_remote_copy(
            src_ref=src, dst_ref=dst, send_sem=send_sem, recv_sem=recv_sem,
            device_id=where, device_id_type=MESH,
        )

    block_rows = proj_in.shape[1]
    row_count = query_buf.shape[0]
    has_prev = jnp.minimum(me, 1)
    has_next = jnp.minimum(count - 1 - me, 1)
    to_prev = {"seq": jnp.maximum(me - 1, 0)}
    to_next = {"seq": jnp.minimum(me + 1, count - 1)}
    own_rows = pl.ds(pl.multiple_of(core * block_rows, LANES), block_rows)
    other_rows = pl.ds(pl.multiple_of(other * block_rows, LANES), block_rows)
    inside = pl.ds(WINDOW, row_count)
    pieces = (
        (key_hbm, key_buf.at[inside]),
        (value_hbm, value_buf.at[inside]),
        (query_hbm, query_buf),
        (o_hbm, o_buf),
        (residual_hbm.at[:, own_rows], residual_buf),
        (gate_hbm.at[0], gate_w),
        (up_hbm.at[0], up_w),
        (down_hbm.at[0], down_w),
    )
    copies = [
        pltpu.make_async_copy(src, dst, local_sem.at[index])
        for index, (src, dst) in enumerate(pieces)
    ]
    for copy in copies[:5]:
        copy.start()
    barrier = pltpu.get_barrier_semaphore()
    pl.semaphore_signal(barrier, inc=1, device_id=to_core, device_id_type=MESH)
    pl.semaphore_signal(barrier, inc=1, device_id=to_pair, device_id_type=MESH)

    @pl.when(has_low == 1)
    def _():
        pl.semaphore_signal(barrier, inc=1, device_id=to_low, device_id_type=MESH)

    @pl.when(has_high == 1)
    def _():
        pl.semaphore_signal(barrier, inc=1, device_id=to_high, device_id_type=MESH)

    @pl.when(has_prev == 1)
    def _():
        pl.semaphore_signal(barrier, inc=1, device_id=to_prev, device_id_type=MESH)

    @pl.when(has_next == 1)
    def _():
        pl.semaphore_signal(barrier, inc=1, device_id=to_next, device_id_type=MESH)

    gain_cols[...] = jnp.broadcast_to(gain_ref[...].reshape(1, -1), (8, feature_dim)).T
    pl.semaphore_wait(barrier, 2 + has_low + has_high + has_prev + has_next)
    for copy in copies[:2]:
        copy.wait()

    def rim_copy(index, buf):
        return send(
            buf.at[pl.ds(row_count, WINDOW)], buf.at[pl.ds(0, WINDOW)],
            rim_send.at[index], rim_recv.at[index], to_next,
        )

    rims = (rim_copy(0, key_buf), rim_copy(1, value_buf))

    @pl.when(has_next == 1)
    def _():
        for copy in rims:
            copy.start()

    copies[2].wait()
    for copy in copies[5:]:
        copy.start()
    attend_block(me, 1, sink_ref, query_buf, key_buf, value_buf, heads)

    @pl.when(has_prev == 1)
    def _():
        for copy in rims:
            copy.wait_recv()

    @pl.when(has_prev == 0)
    def _():
        key_buf[:WINDOW] = jnp.zeros((WINDOW, key_buf.shape[1]), key_buf.dtype)
        value_buf[:WINDOW] = jnp.zeros((WINDOW, value_buf.shape[1]), value_buf.dtype)

    attend_block(me, 0, sink_ref, query_buf, key_buf, value_buf, heads)
    for copy in copies[3:5]:
        copy.wait()

    proj_cuts = cuts_of(feature_dim, proj_send.shape[0])

    def proj_copy(index):
        start, size = proj_cuts[index]
        here = pl.ds(start, size)
        return send(
            proj_out.at[here], proj_in.at[here], proj_send.at[index], proj_recv.at[index], to_core
        )

    both_heads = jnp.concatenate([heads[other_rows, :], heads[own_rows, :]], axis=0)
    for index, (start, size) in enumerate(proj_cuts):
        terms = lax.dot_general(
            o_buf[start : start + size, :], both_heads, (((1,), (1,)), ((), ())),
            preferred_element_type=jnp.float32,
        )
        proj_out[start : start + size, :] = terms[:, :block_rows].astype(jnp.bfloat16)
        proj_copy(index).start()
        stream[start : start + size, :] = (
            residual_buf[start : start + size, :].astype(jnp.float32) + terms[:, block_rows:]
        )
    own_routes = routes_ref[:, own_rows]
    own_codes = codes_ref[:, own_rows].astype(jnp.float32)
    code_rows = rows.shape[2] - feature_dim
    expert = lax.broadcasted_iota(jnp.int32, (code_rows, block_rows), 0)
    spread = jnp.zeros((code_rows, block_rows), jnp.float32)
    for choice in range(TOP):
        named = expert == own_routes[choice : choice + 1, :]
        spread = jnp.where(named, own_codes[choice : choice + 1, :], spread)
    rows[me, core, feature_dim:, :] = spread.astype(jnp.bfloat16)
    spread_sum = jnp.zeros((1, block_rows), jnp.float32)
    for index, (start, size) in enumerate(proj_cuts):
        here = slice(start, start + size)
        proj_copy(index).wait_recv()
        attended = (stream[here, :] + proj_in[here, :].astype(jnp.float32)).astype(jnp.bfloat16)
        attended_ref[here, :] = attended
        widened = attended.astype(jnp.float32)
        spread_sum = spread_sum + jnp.sum(widened * widened, axis=0, keepdims=True)
    scale = lax.rsqrt(spread_sum / feature_dim + 1e-05)
    rows[me, core, :feature_dim, :] = (
        attended_ref[...].astype(jnp.float32) * scale * gain_cols[:, :1]
    ).astype(jnp.bfloat16)

    def absolute(at):
        return base + step * at

    def block_of(at, cross):
        return chip_of(absolute(at), 1 - side if cross else side)

    def row_copy(unit, at, cross, index, kind):
        chip = block_of(at, cross)
        start, size = row_cuts[index]
        slot = rows.at[chip, core, pl.ds(start, size)]
        batch = 6 if kind == 3 else 2 * kind + (at == unit if kind == 1 else cross)
        return send(
            slot, slot, row_send.at[batch],
            others_recv.at[chip] if kind == 3 else row_recv.at[chip, index],
            (to_back, to_pair, to_ahead, to_core)[kind],
        )

    def half_copy(chip):
        return send(
            part.at[chip, other], from_core.at[chip], half_send.at[0], half_recv.at[chip], to_core
        )

    def span(index):
        start, size = piece_cuts[index]
        return pl.ds(start, size)

    def turn_copy(at, index):
        return send(
            part.at[block_of(at, 1), core, span(index)], turn_in.at[absolute(at), span(index)],
            turn_send.at[0], turn_recv.at[absolute(at), turned_pieces.index(index)], to_pair,
        )

    def chain_slot(dest, receiver, sign):
        return jnp.where((dest == receiver) & (sign * step < 0), outer, dest)

    def chain_copy(at, cross, index, sign, receiver=None):
        dest = absolute(at)
        slot = dest if receiver is None else chain_slot(dest, receiver, sign)
        column = len(PIECE_TURNS) + plain_pieces.index(index) if cross else index
        return send(
            part.at[block_of(at, cross), core, span(index)],
            chain_in.at[slot, cross, span(index)],
            chain_send.at[cross], chain_recv.at[slot, column],
            to_ahead if sign > 0 else to_back,
        )

    def cross_copy(unit, index):
        return send(
            part.at[block_of(unit, 1), core, span(index)], cross_in.at[span(index)],
            cross_send.at[0], cross_recv.at[plain_pieces.index(index)], to_pair,
        )

    def compute(chip):
        codes = jnp.concatenate(
            [rows[chip, 0, feature_dim:, :], rows[chip, 1, feature_dim:, :]], axis=1
        ).astype(jnp.float32)
        expert = lax.broadcasted_iota(jnp.int32, codes.shape, 0)
        total = jnp.sum(codes, axis=0, keepdims=True)
        mine = jnp.sum(jnp.where(expert == me, codes, 0.0), axis=0, keepdims=True)
        normed = jnp.concatenate(
            [rows[chip, 0, :feature_dim, :], rows[chip, 1, :feature_dim, :]], axis=1
        )
        gate_val = jnp.dot(gate_t[...], normed, preferred_element_type=jnp.float32)
        up_val = jnp.dot(up_t[...], normed, preferred_element_type=jnp.float32)
        hidden = swiglu(gate_val, up_val).astype(jnp.bfloat16)
        result = jnp.dot(down_t[...], hidden, preferred_element_type=jnp.float32)
        result = (result * (mine / total)).astype(jnp.bfloat16)
        part[chip, 0] = result[:, :block_rows]
        part[chip, 1] = result[:, block_rows:]
        half_copy(chip).start()

    def add_up(dst, sources, index):
        start, size = piece_cuts[index]
        slab = 96 if size % 96 == 0 else 16

        def one(at, carry):
            here = pl.ds(pl.multiple_of(start + at * slab, 16), slab)
            total = sources[0][here, :].astype(jnp.float32)
            for source in sources[1:]:
                total = total + source[here, :].astype(jnp.float32)
            dst[here, :] = total.astype(jnp.bfloat16)
            return carry

        lax.fori_loop(0, size // slab, one, 0)

    def sends_of(unit, task):
        kind, where = task[0], task[1:]
        if kind == RELAY:
            at, cross, index = where
            kinds = [3]
            if at <= unit < outer - 1:
                kinds.append(2)
            if at >= unit > 0:
                kinds.append(0)
            if not cross and (at == unit or not ROW_TURNS[index]):
                kinds.append(1)
            return [functools.partial(row_copy, unit, at, cross, index, way) for way in kinds[::-1]]
        if kind == AWAIT:
            at, index = where
            return [functools.partial(row_copy, unit, at, 1, index, 3)]
        if kind == TURN:
            return [functools.partial(turn_copy, *where)]
        if kind == CHAIN:
            return [functools.partial(chain_copy, *where, line + where[3] * step)]
        if kind == CROSS:
            return [functools.partial(cross_copy, unit, *where)]
        return []

    def arrivals(unit, cross, index):
        chip = block_of(unit, cross)
        sources = [part.at[chip, core], from_core.at[chip]]
        for sign, there in ((1, unit > 0), (-1, unit < outer - 1)):
            if there:
                chain_copy(unit, cross, index, sign, line).wait_recv()
                sources.append(chain_in.at[chain_slot(absolute(unit), line, sign), cross])
        return sources

    def run_task(unit, task):
        kind, where = task[0], task[1:]
        if kind == RELAY and (where[0] != unit or where[1]):
            row_copy(unit, where[0], where[1], where[2], 1).wait_recv()
        if kind == AWAIT:
            row_copy(unit, where[0], 1, where[1], 1).wait_recv()
        if kind == TURN:
            at, index = where
            chip = block_of(at, 1)
            add_up(part.at[chip, core], [part.at[chip, core], from_core.at[chip]], index)
        if kind == CHAIN:
            at, cross, index, sign = where
            chip = block_of(at, cross)
            sources = [part.at[chip, core], from_core.at[chip]]
            if PIECE_TURNS[index] and not cross:
                turn_copy(at, index).wait_recv()
                sources.append(turn_in.at[absolute(at)])
            if (unit if sign > 0 else outer - 1 - unit) > 0:
                chain_copy(at, cross, index, sign).wait_recv()
                sources.append(chain_in.at[absolute(at), cross])
            add_up(part.at[chip, core], sources, index)
        if kind == CROSS:
            sources = arrivals(unit, 1, where[0])
            add_up(part.at[block_of(unit, 1), core], sources, where[0])
        if kind == FINISH:
            index = where[0]
            sources = arrivals(unit, 0, index)
            if PIECE_TURNS[index]:
                turn_copy(unit, index).wait_recv()
                sources.append(turn_in.at[absolute(unit)])
            else:
                cross_copy(unit, index).wait_recv()
                sources.append(cross_in)
            add_up(out_ref, sources, index)
        for make in sends_of(unit, task):
            make().start()

    def all_sent(buf, blocks, extent, sem):
        if blocks * extent:
            sent = buf.at[pl.ds(0, blocks), core, pl.ds(0, extent)]
            pltpu.make_async_copy(sent, sent, sem).wait()

    def plan_of(unit):
        stretches, blocks, seen = [[]], [], set()
        for task in ORDERS[unit]:
            if task[0] == APPLY:
                blocks.append(task[1:])
                stretches.append([])
                continue
            need = {
                TURN: lambda: (task[1], 1),
                CHAIN: lambda: (task[1], task[2]),
                CROSS: lambda: (unit, 1),
                FINISH: lambda: (unit, 0),
            }.get(task[0], lambda: None)()
            fresh = need is not None and need not in seen
            seen.add(need)
            stretches[-1].append((task, need if fresh else None))
        return stretches, blocks

    plans = [plan_of(unit) for unit in range(len(ORDERS))]

    def run_stretch(unit, stretch):
        for task, fresh in stretch:
            if fresh is not None:
                half_copy(block_of(*fresh)).wait_recv()
            run_task(unit, task)

    def one_block(turn, carry):
        at = jnp.int32(0)
        cross = jnp.int32(0)
        for unit, (stretches, blocks) in enumerate(plans):
            for number, (block_at, block_cross) in enumerate(blocks):
                here = (place == unit) & (turn == number)
                at = jnp.where(here, block_at, at)
                cross = jnp.where(here, block_cross, cross)

                @pl.when(here)
                def _(unit=unit, stretch=stretches[number]):
                    run_stretch(unit, stretch)

        @pl.when(turn == 0)
        def _():
            for copy in copies[5:]:
                copy.wait()
            gate_t[...] = gate_w[...].T
            up_t[...] = up_w[...].T
            down_t[...] = down_w[...].T

        chip = chip_of(absolute(at), side + cross * (1 - 2 * side))
        slot = rows.at[chip, other]
        send(slot, slot, row_send.at[6], others_recv.at[chip], to_core).wait_recv()
        compute(chip)
        return carry

    lax.fori_loop(0, count, one_block, 0)
    for unit, (stretches, blocks) in enumerate(plans):
        @pl.when(place == unit)
        def _(unit=unit, stretches=stretches):
            run_stretch(unit, stretches[-1])
            turned_rows = sum(row_cuts[index][1] for index, flag in enumerate(ROW_TURNS) if flag)
            for kind, blocks in ((0, outer - unit if unit else 0), (2, unit + 1)):
                all_sent(rows, blocks, rows.shape[2], row_send.at[2 * kind])
                all_sent(rows, blocks, turned_rows, row_send.at[2 * kind + 1])
            all_sent(rows, 1, rows.shape[2], row_send.at[3])
            all_sent(rows, outer - 1, rows.shape[2] - turned_rows, row_send.at[2])

    first_rows = sum(piece_cuts[index][1] for index in turned_pieces)
    all_sent(rows, count, rows.shape[2], row_send.at[6])
    all_sent(part, count, feature_dim, half_send.at[0])
    all_sent(part, outer, first_rows, turn_send.at[0])
    all_sent(part, 1, feature_dim - first_rows, cross_send.at[0])
    all_sent(part, outer - 1, feature_dim, chain_send.at[0])
    all_sent(part, outer - 1, feature_dim - first_rows, chain_send.at[1])
    for index in range(len(proj_cuts)):
        proj_copy(index).wait_send()

    @pl.when(has_next == 1)
    def _():
        for copy in rims:
            copy.wait_send()


def hand_on(attended_ref, mixture_ref, attended_out, mixture_out, held, came, went):
    arriving = [
        pltpu.make_async_copy(ref, held.at[index], came.at[index])
        for index, ref in enumerate((attended_ref, mixture_ref))
    ]
    leaving = [
        pltpu.make_async_copy(held.at[index], ref, went.at[index])
        for index, ref in enumerate((attended_out, mixture_out))
    ]
    for copy in arriving:
        copy.start()
    for copy, onward in zip(arriving, leaving):
        copy.wait()
        onward.start()
    for copy in leaving:
        copy.wait()


def whole_layer(
    queries, key_rows, values, sink_logit, o_weight, residual, norm_gain, routes, gate_codes,
    w_gate, w_up, w_down,
):
    row_count, feature_dim = residual.shape
    block_rows = row_count // 2
    chips = lax.axis_size("seq")
    outer = chips // INNER
    hidden_dim = w_gate.shape[2]
    turned = (feature_dim, block_rows)
    coded = (feature_dim + CODE_ROWS, block_rows)
    chunks, pieces = len(ROW_TURNS), len(PIECE_TURNS)
    dma = pltpu.SemaphoreType.DMA
    vmem = pl.BlockSpec(memory_space=pltpu.VMEM)
    half = jnp.bfloat16
    attended, mixture = pl.pallas_call(
        layer_kernel,
        out_shape=(jax.ShapeDtypeStruct(turned, half), jax.ShapeDtypeStruct(turned, half)),
        in_specs=[pl.BlockSpec(memory_space=pltpu.SMEM), vmem, vmem, vmem]
        + [pl.BlockSpec(memory_space=pl.ANY)] * 8,
        out_specs=(vmem, vmem),
        scratch_shapes=[
            pltpu.VMEM(queries.shape, half),
            pltpu.VMEM((WINDOW + row_count, key_rows.shape[1]), half),
            pltpu.VMEM((WINDOW + row_count, values.shape[1]), half),
            pltpu.VMEM(o_weight.shape[::-1], half),
            pltpu.VMEM(turned, half),
            pltpu.VMEM(queries.shape, half),
            pltpu.VMEM((feature_dim, 8), jnp.float32),
            pltpu.VMEM(turned, jnp.float32),
            pltpu.VMEM(turned, half),
            pltpu.VMEM(turned, half),
            dma((2,)),
            dma((2,)),
            dma((PROJ_CUTS,)),
            dma((PROJ_CUTS,)),
            pltpu.VMEM((chips, 2) + coded, half),
            pltpu.VMEM((chips, 2) + turned, half),
            pltpu.VMEM((chips,) + turned, half),
            pltpu.VMEM((outer + 1, 2) + turned, half),
            pltpu.VMEM((outer,) + turned, half),
            pltpu.VMEM(turned, half),
            pltpu.VMEM((feature_dim, hidden_dim), half),
            pltpu.VMEM((feature_dim, hidden_dim), half),
            pltpu.VMEM((hidden_dim, feature_dim), half),
            pltpu.VMEM((hidden_dim, feature_dim), half),
            pltpu.VMEM((hidden_dim, feature_dim), half),
            pltpu.VMEM((feature_dim, hidden_dim), half),
            dma((8,)),
            dma((chips, chunks)),
            dma((chips,)),
            dma((7,)),
            dma((1,)),
            dma((chips,)),
            dma((2,)),
            dma((outer + 1, 2 * pieces - sum(PIECE_TURNS))),
            dma((1,)),
            dma((outer, sum(PIECE_TURNS))),
            dma((1,)),
            dma((pieces - sum(PIECE_TURNS),)),
        ],
        compiler_params=pltpu.CompilerParams(
            collective_id=1, has_side_effects=True, vmem_limit_bytes=60 << 20
        ),
    )(
        sink_logit, norm_gain, routes.T, gate_codes.T, queries, key_rows, values,
        o_weight.T, residual.T, w_gate, w_up, w_down,
    )
    attended, mixture = pl.pallas_call(
        hand_on,
        out_shape=(jax.ShapeDtypeStruct(turned, half), jax.ShapeDtypeStruct(turned, half)),
        in_specs=[pl.BlockSpec(memory_space=pl.ANY)] * 2,
        out_specs=(pl.BlockSpec(memory_space=pl.ANY),) * 2,
        scratch_shapes=[pltpu.VMEM((2,) + turned, half), dma((2,)), dma((2,))],
    )(attended, mixture)
    return (attended.T, mixture.T)


def fits_kernel(queries, key_rows, residual, w_gate):
    chips = lax.axis_size("seq")
    return (
        lax.axis_size("exp") == 2
        and chips % INNER == 0
        and chips <= CODE_ROWS
        and residual.shape[1] % 16 == 0
        and chips == 2 * INNER * len(ORDERS)
        and w_gate.shape[0] == 1
        and residual.shape[0] == 2 * WINDOW
        and 2 * TOP >= chips
        and key_rows.shape[1] == LANES
        and queries.shape[1] % (2 * LANES) == 0
    )


def local(
    queries,
    key_rows,
    values,
    sink_logit,
    o_weight,
    residual,
    norm_gain,
    routes,
    gate_codes,
    w_gate,
    w_up,
    w_down,
):
    if fits_kernel(queries, key_rows, residual, w_gate):
        return whole_layer(
            queries, key_rows, values, sink_logit, o_weight, residual, norm_gain, routes,
            gate_codes, w_gate, w_up, w_down,
        )
    heads_out = window_attention(queries, key_rows, values, sink_logit)
    proj_terms = jnp.dot(heads_out, o_weight, preferred_element_type=jnp.float32)
    owners = lax.axis_size("exp")
    owner_pos = lax.axis_index("exp")
    block_rows = residual.shape[0] // owners
    expert_count = w_gate.shape[0] * lax.axis_size("seq")
    capacity = max(2, 2 * block_rows * TOP // expert_count)
    feature_dim = residual.shape[1]
    own_stream = lax.dynamic_slice_in_dim(residual, owner_pos * block_rows, block_rows, 0)
    own_routes = lax.dynamic_slice_in_dim(routes, owner_pos * block_rows, block_rows, 0)
    own_codes = lax.dynamic_slice_in_dim(gate_codes, owner_pos * block_rows, block_rows, 0)
    own_terms = lax.psum_scatter(proj_terms, "exp", scatter_dimension=0, tiled=True)
    attended = (own_stream.astype(jnp.float32) + own_terms).astype(jnp.bfloat16)
    normed = rms_norm(attended, norm_gain)
    outbox, pair_ids, within, shares = pack_rows(
        normed, own_routes, own_codes, expert_count, capacity
    )
    partial_value = expert_apply(
        lax.all_gather(
            lax.all_to_all(
                outbox.reshape(expert_count, capacity, feature_dim),
                "seq",
                split_axis=0,
                concat_axis=0,
                tiled=True,
            ),
            "exp",
            axis=0,
            tiled=True,
        ),
        w_gate,
        w_up,
        w_down,
    )
    whole = lax.psum_scatter(
        partial_value.astype(jnp.bfloat16), "exp", scatter_dimension=0, tiled=True
    ).astype(jnp.float32)
    returned = lax.all_to_all(
        whole.astype(jnp.bfloat16), "seq", split_axis=0, concat_axis=0, tiled=True
    ).astype(whole.dtype)
    picked = returned[pair_ids, within]
    mixture = jnp.sum((picked * shares[:, None]).reshape(-1, TOP, feature_dim), axis=1)
    return (attended, mixture.astype(jnp.bfloat16))


def solution(mesh):
    placed = (
        P(("groups", "seq"), "exp"),
        P(("groups", "seq"), "exp"),
        P(("groups", "seq"), "exp"),
        P("exp"),
        P("exp", None),
        P(("groups", "seq"), None),
        P(),
        P(("groups", "seq"), None),
        P(("groups", "seq"), None),
        P("seq", None, "exp"),
        P("seq", None, "exp"),
        P("seq", "exp", None),
    )
    return jax.shard_map(
        local,
        mesh=mesh,
        in_specs=placed,
        out_specs=(P(("groups", "seq", "exp"), None), P(("groups", "seq", "exp"), None)),
        check_vma=False,
    )
```

```python
import functools

import jax
import jax.numpy as jnp
from jax import lax
from jax.experimental import pallas as pl
from jax.experimental.pallas import tpu as pltpu
from jax.sharding import PartitionSpec as P

HEAD_DIM = 64
WINDOW = 128
TOP = 4


def shifted(value, axis, steps):
    count = lax.axis_size(axis)
    first, last = (max(0, -steps), min(count, count - steps))
    return lax.ppermute(value, axis, [(source, source + steps) for source in range(first, last)])


def swiglu(gate_val, up_val):
    return (up_val + 1.0) * gate_val * (0.5 + 0.5 * jnp.tanh(0.851 * gate_val))


def rms_norm(stream, norm_gain):
    widened = stream.astype(jnp.float32)
    spread = jnp.mean(widened * widened, axis=-1, keepdims=True)
    return (widened * lax.rsqrt(spread + 1e-05) * norm_gain).astype(jnp.bfloat16)


def window_attention(queries, key_rows, values, sink_logit):
    row_count = queries.shape[0]
    kv_local = key_rows.shape[1] // HEAD_DIM
    group_size = queries.shape[1] // HEAD_DIM // kv_local
    rim_keys, rim_values = shifted(
        (key_rows[row_count - WINDOW :], values[row_count - WINDOW :]), "seq", 1
    )
    full_keys = jnp.concatenate([rim_keys, key_rows], axis=0).reshape(
        WINDOW + row_count, kv_local, HEAD_DIM
    )
    full_values = jnp.concatenate([rim_values, values], axis=0).reshape(
        WINDOW + row_count, kv_local, HEAD_DIM
    )
    grouped = queries.reshape(row_count, kv_local, group_size, HEAD_DIM)
    scores = jnp.einsum(
        "tgjd,ugd->gjtu", grouped, full_keys, preferred_element_type=jnp.float32
    ) * HEAD_DIM ** (-0.5)
    query_pos = jnp.arange(row_count, dtype=jnp.int32)[:, None] + WINDOW
    key_pos = jnp.arange(WINDOW + row_count, dtype=jnp.int32)[None, :]
    first_key = jnp.where(lax.axis_index("seq") == 0, WINDOW, 0)
    allowed = (key_pos <= query_pos) & (key_pos > query_pos - WINDOW) & (key_pos >= first_key)
    scores = jnp.where(allowed, scores, -1e30)
    sink_vals = sink_logit.reshape(kv_local, group_size)[:, :, None, None]
    ceiling = jnp.maximum(jnp.max(scores, axis=-1, keepdims=True), sink_vals)
    raised = jnp.exp(scores - ceiling)
    denominator = jnp.sum(raised, axis=-1, keepdims=True) + jnp.exp(sink_vals - ceiling)
    weights = (raised / denominator).astype(jnp.bfloat16)
    mixed = jnp.einsum("gjtu,ugd->tgjd", weights, full_values, preferred_element_type=jnp.float32)
    return mixed.astype(jnp.bfloat16).reshape(row_count, kv_local * group_size * HEAD_DIM)


def pack_rows(normed, expert_ids, gate_codes, expert_count, capacity):
    pair_ids = expert_ids.reshape(-1)
    matches = (pair_ids[:, None] == jnp.arange(expert_count, dtype=jnp.int32)[None, :]).astype(
        jnp.float32
    )
    order = jnp.arange(pair_ids.shape[0], dtype=jnp.int32)
    earlier = (order[:, None] > order[None, :]).astype(jnp.bfloat16)
    before = jnp.dot(earlier, matches.astype(jnp.bfloat16), preferred_element_type=jnp.float32)
    within = jnp.sum(before * matches, axis=1).astype(jnp.int32)
    sources = normed[jnp.arange(pair_ids.shape[0], dtype=jnp.int32) // expert_ids.shape[1]]
    outbox = jnp.zeros((expert_count * capacity, normed.shape[1]), normed.dtype)
    outbox = outbox.at[pair_ids * capacity + within].set(sources)
    code_vals = gate_codes.astype(jnp.float32)
    shares = (code_vals / jnp.sum(code_vals, axis=1, keepdims=True)).reshape(-1)
    return (outbox, pair_ids, within, shares)


def expert_apply(arrived, w_gate, w_up, w_down):
    flat_rows = arrived.reshape(-1, arrived.shape[-1])
    gate_val = jnp.dot(flat_rows, w_gate[0], preferred_element_type=jnp.float32)
    up_val = jnp.dot(flat_rows, w_up[0], preferred_element_type=jnp.float32)
    hidden = swiglu(gate_val, up_val).astype(jnp.bfloat16)
    result = jnp.dot(hidden, w_down[0], preferred_element_type=jnp.float32)
    return result.reshape(arrived.shape)


LANES = 128
INNER = 2
CODE_ROWS = 16
PROJ_CUTS = 3
RELAY, AWAIT, APPLY, TURN, CHAIN, CROSS, FINISH = range(7)
ROW_TURNS = (0, 0, 0, 1)
PIECE_TURNS = (1, 1, 0, 0)
ORDERS = (
    (
        (RELAY, 0, 0, 0), (RELAY, 0, 0, 2), (RELAY, 0, 0, 3), (RELAY, 0, 0, 1), (RELAY, 1, 0, 3),
        (RELAY, 1, 0, 1), (RELAY, 1, 0, 2), (APPLY, 0, 0), (RELAY, 0, 1, 3), (AWAIT, 0, 1),
        (RELAY, 1, 0, 0), (RELAY, 2, 0, 2), (AWAIT, 1, 2), (APPLY, 1, 0), (CHAIN, 1, 0, 2, 1),
        (RELAY, 1, 1, 3), (AWAIT, 1, 0), (RELAY, 2, 0, 1), (CHAIN, 1, 0, 3, 1), (AWAIT, 1, 1),
        (RELAY, 3, 0, 0), (AWAIT, 0, 2), (APPLY, 1, 1), (RELAY, 2, 0, 3), (RELAY, 2, 0, 0),
        (RELAY, 3, 0, 1), (AWAIT, 3, 0), (CHAIN, 1, 1, 3, 1), (AWAIT, 2, 2), (APPLY, 2, 0),
        (RELAY, 3, 0, 2), (CHAIN, 1, 1, 2, 1), (RELAY, 2, 1, 3), (AWAIT, 2, 1), (AWAIT, 2, 0),
        (CHAIN, 2, 0, 2, 1), (CHAIN, 2, 0, 3, 1), (APPLY, 2, 1), (AWAIT, 3, 1), (RELAY, 3, 1, 3),
        (TURN, 1, 1), (AWAIT, 3, 2), (CHAIN, 2, 1, 2, 1), (APPLY, 3, 1), (RELAY, 3, 0, 3),
        (CHAIN, 2, 1, 3, 1), (TURN, 3, 0), (CHAIN, 3, 1, 2, 1), (CHAIN, 3, 1, 3, 1), (APPLY, 3, 0),
        (TURN, 3, 1), (TURN, 1, 0), (CHAIN, 3, 0, 2, 1), (CHAIN, 3, 0, 0, 1), (TURN, 2, 1),
        (AWAIT, 0, 0), (TURN, 2, 0), (CHAIN, 3, 0, 3, 1), (APPLY, 0, 1), (CHAIN, 3, 0, 1, 1),
        (CHAIN, 2, 0, 1, 1), (TURN, 0, 1), (CROSS, 2), (CHAIN, 2, 0, 0, 1), (CROSS, 3),
        (CHAIN, 1, 0, 0, 1), (TURN, 0, 0), (FINISH, 2), (CHAIN, 1, 0, 1, 1), (FINISH, 0), (FINISH, 3),
        (FINISH, 1),
    ),
    (
        (RELAY, 1, 0, 3), (RELAY, 1, 0, 1), (RELAY, 1, 0, 2), (RELAY, 1, 0, 0), (RELAY, 1, 1, 3),
        (APPLY, 1, 0), (RELAY, 2, 0, 2), (RELAY, 2, 0, 1), (AWAIT, 1, 1), (RELAY, 0, 0, 0),
        (AWAIT, 1, 0), (RELAY, 0, 0, 1), (RELAY, 0, 0, 2), (AWAIT, 1, 2), (RELAY, 2, 0, 0),
        (APPLY, 1, 1), (RELAY, 3, 0, 0), (RELAY, 0, 1, 3), (RELAY, 2, 0, 3), (RELAY, 3, 0, 1),
        (RELAY, 0, 0, 3), (AWAIT, 2, 2), (APPLY, 2, 0), (APPLY, 0, 0), (RELAY, 3, 0, 2), (AWAIT, 2, 0),
        (RELAY, 2, 1, 3), (AWAIT, 2, 1), (RELAY, 3, 1, 3), (APPLY, 2, 1), (AWAIT, 0, 1), (AWAIT, 3, 1),
        (AWAIT, 3, 0), (AWAIT, 3, 2), (TURN, 2, 0), (AWAIT, 0, 0), (RELAY, 3, 0, 3), (APPLY, 3, 1),
        (TURN, 2, 1), (APPLY, 3, 0), (AWAIT, 0, 2), (CHAIN, 2, 0, 2, 1), (CHAIN, 2, 0, 3, 1),
        (APPLY, 0, 1), (TURN, 3, 0), (CHAIN, 2, 1, 2, 1), (CHAIN, 2, 1, 3, 1), (TURN, 0, 1),
        (CHAIN, 3, 1, 2, 1), (TURN, 3, 1), (CHAIN, 3, 1, 3, 1), (CROSS, 2), (TURN, 0, 0), (TURN, 1, 1),
        (CHAIN, 3, 0, 2, 1), (CHAIN, 0, 1, 2, -1), (CHAIN, 3, 0, 0, 1), (CHAIN, 0, 1, 3, -1),
        (CHAIN, 3, 0, 3, 1), (TURN, 1, 0), (CHAIN, 0, 0, 2, -1), (CROSS, 3), (CHAIN, 3, 0, 1, 1),
        (CHAIN, 0, 0, 0, -1), (FINISH, 2), (CHAIN, 2, 0, 1, 1), (CHAIN, 0, 0, 3, -1),
        (CHAIN, 2, 0, 0, 1), (CHAIN, 0, 0, 1, -1), (FINISH, 3), (FINISH, 0), (FINISH, 1),
    ),
)


def cuts_of(extent, parts):
    edges = [extent // 16 * part // parts * 16 for part in range(parts)] + [extent]
    return [(first, last - first) for first, last in zip(edges, edges[1:])]
MESH = pl.DeviceIdType.MESH


def attend_block(me, block, sink_ref, query_buf, key_buf, value_buf, heads):
    start = block * WINDOW
    lane = lax.broadcasted_iota(jnp.int32, (2 * WINDOW, LANES), 1)
    query_pos = lax.broadcasted_iota(jnp.int32, (WINDOW, WINDOW), 0)
    key_pos = lax.broadcasted_iota(jnp.int32, (WINDOW, WINDOW), 1)
    recent = key_pos <= query_pos
    opening = (me == 0) & (block == 0)

    def halves(buf, head):
        plain = buf[start : start + 2 * WINDOW, :].astype(jnp.float32)
        turned = pltpu.roll(plain, HEAD_DIM, axis=1)
        low, high = (plain, turned) if head == 0 else (turned, plain)
        return jnp.concatenate(
            [jnp.where(lane < HEAD_DIM, low, 0.0), jnp.where(lane < HEAD_DIM, 0.0, high)], axis=0
        ).astype(jnp.bfloat16)

    pairs = query_buf.shape[1] // LANES
    for head in range(2):
        both_keys = halves(key_buf, head) * jnp.bfloat16(HEAD_DIM ** (-0.5))
        both_values = halves(value_buf, head)
        for pair in range(head * pairs // 2, (head + 1) * pairs // 2):
            columns = slice(pair * LANES, (pair + 1) * LANES)
            scores = lax.dot_general(
                query_buf[start : start + WINDOW, columns], both_keys,
                (((1,), (1,)), ((), ())), preferred_element_type=jnp.float32,
            )
            weights = []
            for half in range(2):
                sink = sink_ref[2 * pair + half]
                first = 2 * half * WINDOW
                earlier = scores[:, first : first + WINDOW]
                if block == 0:
                    earlier = jnp.where(opening, -1e30, earlier)
                seen = jnp.where(recent, scores[:, first + WINDOW : first + 2 * WINDOW], earlier)
                ceiling = jnp.maximum(jnp.max(seen, axis=1, keepdims=True), sink)
                raised = jnp.exp(seen - ceiling)
                below = jnp.sum(raised, axis=1, keepdims=True) + jnp.exp(sink - ceiling)
                shares = raised * (1.0 / below)
                weights.append(jnp.where(recent, 0.0, shares).astype(jnp.bfloat16))
                weights.append(jnp.where(recent, shares, 0.0).astype(jnp.bfloat16))
            mixed = jnp.dot(
                jnp.concatenate(weights, axis=1), both_values, preferred_element_type=jnp.float32
            )
            heads[start : start + WINDOW, columns] = mixed.astype(jnp.bfloat16)


def layer_kernel(
    sink_ref, gain_ref, routes_ref, codes_ref, query_hbm, key_hbm, value_hbm,
    o_hbm, residual_hbm, gate_hbm, up_hbm, down_hbm, attended_ref, out_ref,
    query_buf, key_buf, value_buf, o_buf, residual_buf, heads, gain_cols, stream, proj_out, proj_in,
    rim_send, rim_recv, proj_send, proj_recv, rows, part, from_core, chain_in, turn_in, cross_in,
    gate_w, up_w, down_w, gate_t, up_t, down_t,
    local_sem, row_recv, others_recv, row_send, half_send, half_recv, chain_send, chain_recv,
    turn_send, turn_recv, cross_send, cross_recv,
):
    me = lax.axis_index("seq")
    core = lax.axis_index("exp")
    other = 1 - core
    count = lax.axis_size("seq")
    outer = count // INNER
    line = me // INNER
    side = me % INNER
    has_low = jnp.minimum(line, 1)
    has_high = jnp.minimum(outer - 1 - line, 1)
    to_core = {"exp": other}
    to_pair = {"seq": line * INNER + 1 - side}
    to_high = {"seq": jnp.minimum(line + 1, outer - 1) * INNER + side}
    to_low = {"seq": jnp.maximum(line - 1, 0) * INNER + side}
    feature_dim = attended_ref.shape[0]
    flip = 2 * line // outer
    step = 1 - 2 * flip
    base = flip * (outer - 1)
    place = base + step * line
    to_ahead = {"seq": jnp.clip(line + step, 0, outer - 1) * INNER + side}
    to_back = {"seq": jnp.clip(line - step, 0, outer - 1) * INNER + side}
    row_cuts = cuts_of(rows.shape[2], len(ROW_TURNS))
    piece_cuts = cuts_of(feature_dim, len(PIECE_TURNS))
    turned_pieces = [index for index, flag in enumerate(PIECE_TURNS) if flag]
    plain_pieces = [index for index, flag in enumerate(PIECE_TURNS) if not flag]

    def chip_of(at, at_side):
        return at * INNER + at_side

    def send(src, dst, send_sem, recv_sem, where):
        return pltpu.make_async_remote_copy(
            src_ref=src, dst_ref=dst, send_sem=send_sem, recv_sem=recv_sem,
            device_id=where, device_id_type=MESH,
        )

    block_rows = proj_in.shape[1]
    row_count = query_buf.shape[0]
    has_prev = jnp.minimum(me, 1)
    has_next = jnp.minimum(count - 1 - me, 1)
    to_prev = {"seq": jnp.maximum(me - 1, 0)}
    to_next = {"seq": jnp.minimum(me + 1, count - 1)}
    own_rows = pl.ds(pl.multiple_of(core * block_rows, LANES), block_rows)
    other_rows = pl.ds(pl.multiple_of(other * block_rows, LANES), block_rows)
    inside = pl.ds(WINDOW, row_count)
    pieces = (
        (key_hbm, key_buf.at[inside]),
        (value_hbm, value_buf.at[inside]),
        (query_hbm, query_buf),
        (o_hbm, o_buf),
        (residual_hbm.at[:, own_rows], residual_buf),
        (gate_hbm.at[0], gate_w),
        (up_hbm.at[0], up_w),
        (down_hbm.at[0], down_w),
    )
    copies = [
        pltpu.make_async_copy(src, dst, local_sem.at[index])
        for index, (src, dst) in enumerate(pieces)
    ]
    for copy in copies[:5]:
        copy.start()
    barrier = pltpu.get_barrier_semaphore()
    pl.semaphore_signal(barrier, inc=1, device_id=to_core, device_id_type=MESH)
    pl.semaphore_signal(barrier, inc=1, device_id=to_pair, device_id_type=MESH)

    @pl.when(has_low == 1)
    def _():
        pl.semaphore_signal(barrier, inc=1, device_id=to_low, device_id_type=MESH)

    @pl.when(has_high == 1)
    def _():
        pl.semaphore_signal(barrier, inc=1, device_id=to_high, device_id_type=MESH)

    @pl.when(has_prev == 1)
    def _():
        pl.semaphore_signal(barrier, inc=1, device_id=to_prev, device_id_type=MESH)

    @pl.when(has_next == 1)
    def _():
        pl.semaphore_signal(barrier, inc=1, device_id=to_next, device_id_type=MESH)

    gain_cols[...] = jnp.broadcast_to(gain_ref[...].reshape(1, -1), (8, feature_dim)).T
    pl.semaphore_wait(barrier, 2 + has_low + has_high + has_prev + has_next)
    for copy in copies[:2]:
        copy.wait()

    def rim_copy(index, buf):
        return send(
            buf.at[pl.ds(row_count, WINDOW)], buf.at[pl.ds(0, WINDOW)],
            rim_send.at[index], rim_recv.at[index], to_next,
        )

    rims = (rim_copy(0, key_buf), rim_copy(1, value_buf))

    @pl.when(has_next == 1)
    def _():
        for copy in rims:
            copy.start()

    copies[2].wait()
    for copy in copies[5:]:
        copy.start()
    attend_block(me, 1, sink_ref, query_buf, key_buf, value_buf, heads)

    @pl.when(has_prev == 1)
    def _():
        for copy in rims:
            copy.wait_recv()

    @pl.when(has_prev == 0)
    def _():
        key_buf[:WINDOW] = jnp.zeros((WINDOW, key_buf.shape[1]), key_buf.dtype)
        value_buf[:WINDOW] = jnp.zeros((WINDOW, value_buf.shape[1]), value_buf.dtype)

    attend_block(me, 0, sink_ref, query_buf, key_buf, value_buf, heads)
    for copy in copies[3:5]:
        copy.wait()

    proj_cuts = cuts_of(feature_dim, proj_send.shape[0])

    def proj_copy(index):
        start, size = proj_cuts[index]
        here = pl.ds(start, size)
        return send(
            proj_out.at[here], proj_in.at[here], proj_send.at[index], proj_recv.at[index], to_core
        )

    both_heads = jnp.concatenate([heads[other_rows, :], heads[own_rows, :]], axis=0)
    for index, (start, size) in enumerate(proj_cuts):
        terms = lax.dot_general(
            o_buf[start : start + size, :], both_heads, (((1,), (1,)), ((), ())),
            preferred_element_type=jnp.float32,
        )
        proj_out[start : start + size, :] = terms[:, :block_rows].astype(jnp.bfloat16)
        proj_copy(index).start()
        stream[start : start + size, :] = (
            residual_buf[start : start + size, :].astype(jnp.float32) + terms[:, block_rows:]
        )
    own_routes = routes_ref[:, own_rows]
    own_codes = codes_ref[:, own_rows].astype(jnp.float32)
    code_rows = rows.shape[2] - feature_dim
    expert = lax.broadcasted_iota(jnp.int32, (code_rows, block_rows), 0)
    spread = jnp.zeros((code_rows, block_rows), jnp.float32)
    for choice in range(TOP):
        named = expert == own_routes[choice : choice + 1, :]
        spread = jnp.where(named, own_codes[choice : choice + 1, :], spread)
    rows[me, core, feature_dim:, :] = spread.astype(jnp.bfloat16)
    spread_sum = jnp.zeros((1, block_rows), jnp.float32)
    for index, (start, size) in enumerate(proj_cuts):
        here = slice(start, start + size)
        proj_copy(index).wait_recv()
        attended = (stream[here, :] + proj_in[here, :].astype(jnp.float32)).astype(jnp.bfloat16)
        attended_ref[here, :] = attended
        widened = attended.astype(jnp.float32)
        spread_sum = spread_sum + jnp.sum(widened * widened, axis=0, keepdims=True)
    scale = lax.rsqrt(spread_sum / feature_dim + 1e-05)
    rows[me, core, :feature_dim, :] = (
        attended_ref[...].astype(jnp.float32) * scale * gain_cols[:, :1]
    ).astype(jnp.bfloat16)

    def absolute(at):
        return base + step * at

    def block_of(at, cross):
        return chip_of(absolute(at), 1 - side if cross else side)

    def row_copy(unit, at, cross, index, kind):
        chip = block_of(at, cross)
        start, size = row_cuts[index]
        slot = rows.at[chip, core, pl.ds(start, size)]
        batch = 6 if kind == 3 else 2 * kind + (at == unit if kind == 1 else cross)
        return send(
            slot, slot, row_send.at[batch],
            others_recv.at[chip] if kind == 3 else row_recv.at[chip, index],
            (to_back, to_pair, to_ahead, to_core)[kind],
        )

    def half_copy(chip):
        return send(
            part.at[chip, other], from_core.at[chip], half_send.at[0], half_recv.at[chip], to_core
        )

    def span(index):
        start, size = piece_cuts[index]
        return pl.ds(start, size)

    def turn_copy(at, index):
        return send(
            part.at[block_of(at, 1), core, span(index)], turn_in.at[absolute(at), span(index)],
            turn_send.at[0], turn_recv.at[absolute(at), turned_pieces.index(index)], to_pair,
        )

    def chain_slot(dest, receiver, sign):
        return jnp.where((dest == receiver) & (sign * step < 0), outer, dest)

    def chain_copy(at, cross, index, sign, receiver=None):
        dest = absolute(at)
        slot = dest if receiver is None else chain_slot(dest, receiver, sign)
        column = len(PIECE_TURNS) + plain_pieces.index(index) if cross else index
        return send(
            part.at[block_of(at, cross), core, span(index)],
            chain_in.at[slot, cross, span(index)],
            chain_send.at[cross], chain_recv.at[slot, column],
            to_ahead if sign > 0 else to_back,
        )

    def cross_copy(unit, index):
        return send(
            part.at[block_of(unit, 1), core, span(index)], cross_in.at[span(index)],
            cross_send.at[0], cross_recv.at[plain_pieces.index(index)], to_pair,
        )

    def compute(chip):
        codes = jnp.concatenate(
            [rows[chip, 0, feature_dim:, :], rows[chip, 1, feature_dim:, :]], axis=1
        ).astype(jnp.float32)
        expert = lax.broadcasted_iota(jnp.int32, codes.shape, 0)
        total = jnp.sum(codes, axis=0, keepdims=True)
        mine = jnp.sum(jnp.where(expert == me, codes, 0.0), axis=0, keepdims=True)
        normed = jnp.concatenate(
            [rows[chip, 0, :feature_dim, :], rows[chip, 1, :feature_dim, :]], axis=1
        )
        parts = []
        for start, size in cuts_of(gate_t.shape[0], 3):
            here = slice(start, start + size)
            gate_val = jnp.dot(gate_t[here, :], normed, preferred_element_type=jnp.float32)
            up_val = jnp.dot(up_t[here, :], normed, preferred_element_type=jnp.float32)
            parts.append(swiglu(gate_val, up_val).astype(jnp.bfloat16))
        hidden = jnp.concatenate(parts, axis=0)
        share = mine / total
        for start, size in cuts_of(feature_dim, 3):
            here = slice(start, start + size)
            result = jnp.dot(down_t[here, :], hidden, preferred_element_type=jnp.float32)
            result = (result * share).astype(jnp.bfloat16)
            part[chip, 0, here, :] = result[:, :block_rows]
            part[chip, 1, here, :] = result[:, block_rows:]
        half_copy(chip).start()

    def add_up(dst, sources, index):
        start, size = piece_cuts[index]
        slab = next((width for width in (96, 80, 112) if size % width == 0), size)

        def one(at, carry):
            here = pl.ds(pl.multiple_of(start + at * slab, 16), slab)
            total = sources[0][here, :].astype(jnp.float32)
            for source in sources[1:]:
                total = total + source[here, :].astype(jnp.float32)
            dst[here, :] = total.astype(jnp.bfloat16)
            return carry

        lax.fori_loop(0, size // slab, one, 0)

    def sends_of(unit, task):
        kind, where = task[0], task[1:]
        if kind == RELAY:
            at, cross, index = where
            kinds = [3]
            if at <= unit < outer - 1:
                kinds.append(2)
            if at >= unit > 0:
                kinds.append(0)
            if not cross and (at == unit or not ROW_TURNS[index]):
                kinds.append(1)
            return [functools.partial(row_copy, unit, at, cross, index, way) for way in kinds[::-1]]
        if kind == AWAIT:
            at, index = where
            return [functools.partial(row_copy, unit, at, 1, index, 3)]
        if kind == TURN:
            return [functools.partial(turn_copy, *where)]
        if kind == CHAIN:
            return [functools.partial(chain_copy, *where, line + where[3] * step)]
        if kind == CROSS:
            return [functools.partial(cross_copy, unit, *where)]
        return []

    def arrivals(unit, cross, index):
        chip = block_of(unit, cross)
        sources = [part.at[chip, core], from_core.at[chip]]
        for sign, there in ((1, unit > 0), (-1, unit < outer - 1)):
            if there:
                chain_copy(unit, cross, index, sign, line).wait_recv()
                sources.append(chain_in.at[chain_slot(absolute(unit), line, sign), cross])
        return sources

    def run_task(unit, task):
        kind, where = task[0], task[1:]
        if kind == RELAY and (where[0] != unit or where[1]):
            row_copy(unit, where[0], where[1], where[2], 1).wait_recv()
        if kind == AWAIT:
            row_copy(unit, where[0], 1, where[1], 1).wait_recv()
        if kind == TURN:
            at, index = where
            chip = block_of(at, 1)
            add_up(part.at[chip, core], [part.at[chip, core], from_core.at[chip]], index)
        if kind == CHAIN:
            at, cross, index, sign = where
            chip = block_of(at, cross)
            sources = [part.at[chip, core], from_core.at[chip]]
            if PIECE_TURNS[index] and not cross:
                turn_copy(at, index).wait_recv()
                sources.append(turn_in.at[absolute(at)])
            if (unit if sign > 0 else outer - 1 - unit) > 0:
                chain_copy(at, cross, index, sign).wait_recv()
                sources.append(chain_in.at[absolute(at), cross])
            add_up(part.at[chip, core], sources, index)
        if kind == CROSS:
            sources = arrivals(unit, 1, where[0])
            add_up(part.at[block_of(unit, 1), core], sources, where[0])
        if kind == FINISH:
            index = where[0]
            sources = arrivals(unit, 0, index)
            if PIECE_TURNS[index]:
                turn_copy(unit, index).wait_recv()
                sources.append(turn_in.at[absolute(unit)])
            else:
                cross_copy(unit, index).wait_recv()
                sources.append(cross_in)
            add_up(out_ref, sources, index)
        for make in sends_of(unit, task):
            make().start()

    def all_sent(buf, blocks, extent, sem):
        if blocks * extent:
            sent = buf.at[pl.ds(0, blocks), core, pl.ds(0, extent)]
            pltpu.make_async_copy(sent, sent, sem).wait()

    def plan_of(unit):
        stretches, blocks, seen = [[]], [], set()
        for task in ORDERS[unit]:
            if task[0] == APPLY:
                blocks.append(task[1:])
                stretches.append([])
                continue
            need = {
                TURN: lambda: (task[1], 1),
                CHAIN: lambda: (task[1], task[2]),
                CROSS: lambda: (unit, 1),
                FINISH: lambda: (unit, 0),
            }.get(task[0], lambda: None)()
            fresh = need is not None and need not in seen
            seen.add(need)
            stretches[-1].append((task, need if fresh else None))
        return stretches, blocks

    plans = [plan_of(unit) for unit in range(len(ORDERS))]

    def run_stretch(unit, stretch):
        for task, fresh in stretch:
            if fresh is not None:
                half_copy(block_of(*fresh)).wait_recv()
            run_task(unit, task)

    def one_block(turn, carry):
        at = jnp.int32(0)
        cross = jnp.int32(0)
        for unit, (stretches, blocks) in enumerate(plans):
            for number, (block_at, block_cross) in enumerate(blocks):
                here = (place == unit) & (turn == number)
                at = jnp.where(here, block_at, at)
                cross = jnp.where(here, block_cross, cross)

                @pl.when(here)
                def _(unit=unit, stretch=stretches[number]):
                    run_stretch(unit, stretch)

        @pl.when(turn == 0)
        def _():
            for copy in copies[5:]:
                copy.wait()
            gate_t[...] = gate_w[...].T
            up_t[...] = up_w[...].T
            down_t[...] = down_w[...].T

        chip = chip_of(absolute(at), side + cross * (1 - 2 * side))
        slot = rows.at[chip, other]
        send(slot, slot, row_send.at[6], others_recv.at[chip], to_core).wait_recv()
        compute(chip)
        return carry

    lax.fori_loop(0, count, one_block, 0)
    for unit, (stretches, blocks) in enumerate(plans):
        @pl.when(place == unit)
        def _(unit=unit, stretches=stretches):
            run_stretch(unit, stretches[-1])
            turned_rows = sum(row_cuts[index][1] for index, flag in enumerate(ROW_TURNS) if flag)
            for kind, blocks in ((0, outer - unit if unit else 0), (2, unit + 1)):
                all_sent(rows, blocks, rows.shape[2], row_send.at[2 * kind])
                all_sent(rows, blocks, turned_rows, row_send.at[2 * kind + 1])
            all_sent(rows, 1, rows.shape[2], row_send.at[3])
            all_sent(rows, outer - 1, rows.shape[2] - turned_rows, row_send.at[2])

    first_rows = sum(piece_cuts[index][1] for index in turned_pieces)
    all_sent(rows, count, rows.shape[2], row_send.at[6])
    all_sent(part, count, feature_dim, half_send.at[0])
    all_sent(part, outer, first_rows, turn_send.at[0])
    all_sent(part, 1, feature_dim - first_rows, cross_send.at[0])
    all_sent(part, outer - 1, feature_dim, chain_send.at[0])
    all_sent(part, outer - 1, feature_dim - first_rows, chain_send.at[1])
    for index in range(len(proj_cuts)):
        proj_copy(index).wait_send()

    @pl.when(has_next == 1)
    def _():
        for copy in rims:
            copy.wait_send()


def hand_on(attended_ref, mixture_ref, attended_out, mixture_out, went):
    copies = [
        pltpu.make_async_copy(attended_ref, attended_out, went.at[0]),
        pltpu.make_async_copy(mixture_ref, mixture_out, went.at[1]),
    ]
    for copy in copies:
        copy.start()
    for copy in copies:
        copy.wait()


def whole_layer(
    queries, key_rows, values, sink_logit, o_weight, residual, norm_gain, routes, gate_codes,
    w_gate, w_up, w_down,
):
    row_count, feature_dim = residual.shape
    block_rows = row_count // 2
    chips = lax.axis_size("seq")
    outer = chips // INNER
    hidden_dim = w_gate.shape[2]
    turned = (feature_dim, block_rows)
    coded = (feature_dim + CODE_ROWS, block_rows)
    chunks, pieces = len(ROW_TURNS), len(PIECE_TURNS)
    dma = pltpu.SemaphoreType.DMA
    vmem = pl.BlockSpec(memory_space=pltpu.VMEM)
    half = jnp.bfloat16
    attended, mixture = pl.pallas_call(
        layer_kernel,
        out_shape=(pltpu.VMEM(turned, half), pltpu.VMEM(turned, half)),
        in_specs=[pl.BlockSpec(memory_space=pltpu.SMEM), vmem, vmem, vmem]
        + [pl.BlockSpec(memory_space=pl.ANY)] * 8,
        out_specs=(vmem, vmem),
        scratch_shapes=[
            pltpu.VMEM(queries.shape, half),
            pltpu.VMEM((WINDOW + row_count, key_rows.shape[1]), half),
            pltpu.VMEM((WINDOW + row_count, values.shape[1]), half),
            pltpu.VMEM(o_weight.shape[::-1], half),
            pltpu.VMEM(turned, half),
            pltpu.VMEM(queries.shape, half),
            pltpu.VMEM((feature_dim, 8), jnp.float32),
            pltpu.VMEM(turned, jnp.float32),
            pltpu.VMEM(turned, half),
            pltpu.VMEM(turned, half),
            dma((2,)),
            dma((2,)),
            dma((PROJ_CUTS,)),
            dma((PROJ_CUTS,)),
            pltpu.VMEM((chips, 2) + coded, half),
            pltpu.VMEM((chips, 2) + turned, half),
            pltpu.VMEM((chips,) + turned, half),
            pltpu.VMEM((outer + 1, 2) + turned, half),
            pltpu.VMEM((outer,) + turned, half),
            pltpu.VMEM(turned, half),
            pltpu.VMEM((feature_dim, hidden_dim), half),
            pltpu.VMEM((feature_dim, hidden_dim), half),
            pltpu.VMEM((hidden_dim, feature_dim), half),
            pltpu.VMEM((hidden_dim, feature_dim), half),
            pltpu.VMEM((hidden_dim, feature_dim), half),
            pltpu.VMEM((feature_dim, hidden_dim), half),
            dma((8,)),
            dma((chips, chunks)),
            dma((chips,)),
            dma((7,)),
            dma((1,)),
            dma((chips,)),
            dma((2,)),
            dma((outer + 1, 2 * pieces - sum(PIECE_TURNS))),
            dma((1,)),
            dma((outer, sum(PIECE_TURNS))),
            dma((1,)),
            dma((pieces - sum(PIECE_TURNS),)),
        ],
        compiler_params=pltpu.CompilerParams(
            collective_id=1, has_side_effects=True, vmem_limit_bytes=60 << 20
        ),
    )(
        sink_logit, norm_gain, routes.T, gate_codes.T, queries, key_rows, values,
        o_weight.T, residual.T, w_gate, w_up, w_down,
    )
    attended, mixture = pl.pallas_call(
        hand_on,
        out_shape=(jax.ShapeDtypeStruct(turned, half), jax.ShapeDtypeStruct(turned, half)),
        in_specs=[vmem] * 2,
        out_specs=(pl.BlockSpec(memory_space=pl.ANY),) * 2,
        scratch_shapes=[dma((2,))],
    )(*(pltpu.with_memory_space_constraint(value, pltpu.VMEM) for value in (attended, mixture)))
    return (attended.T, mixture.T)


def fits_kernel(queries, key_rows, residual, w_gate):
    chips = lax.axis_size("seq")
    return (
        lax.axis_size("exp") == 2
        and chips % INNER == 0
        and chips <= CODE_ROWS
        and residual.shape[1] % 16 == 0
        and chips == 2 * INNER * len(ORDERS)
        and w_gate.shape[0] == 1
        and residual.shape[0] == 2 * WINDOW
        and 2 * TOP >= chips
        and key_rows.shape[1] == LANES
        and queries.shape[1] % (2 * LANES) == 0
    )


def local(
    queries,
    key_rows,
    values,
    sink_logit,
    o_weight,
    residual,
    norm_gain,
    routes,
    gate_codes,
    w_gate,
    w_up,
    w_down,
):
    if fits_kernel(queries, key_rows, residual, w_gate):
        return whole_layer(
            queries, key_rows, values, sink_logit, o_weight, residual, norm_gain, routes,
            gate_codes, w_gate, w_up, w_down,
        )
    heads_out = window_attention(queries, key_rows, values, sink_logit)
    proj_terms = jnp.dot(heads_out, o_weight, preferred_element_type=jnp.float32)
    owners = lax.axis_size("exp")
    owner_pos = lax.axis_index("exp")
    block_rows = residual.shape[0] // owners
    expert_count = w_gate.shape[0] * lax.axis_size("seq")
    capacity = max(2, 2 * block_rows * TOP // expert_count)
    feature_dim = residual.shape[1]
    own_stream = lax.dynamic_slice_in_dim(residual, owner_pos * block_rows, block_rows, 0)
    own_routes = lax.dynamic_slice_in_dim(routes, owner_pos * block_rows, block_rows, 0)
    own_codes = lax.dynamic_slice_in_dim(gate_codes, owner_pos * block_rows, block_rows, 0)
    own_terms = lax.psum_scatter(proj_terms, "exp", scatter_dimension=0, tiled=True)
    attended = (own_stream.astype(jnp.float32) + own_terms).astype(jnp.bfloat16)
    normed = rms_norm(attended, norm_gain)
    outbox, pair_ids, within, shares = pack_rows(
        normed, own_routes, own_codes, expert_count, capacity
    )
    partial_value = expert_apply(
        lax.all_gather(
            lax.all_to_all(
                outbox.reshape(expert_count, capacity, feature_dim),
                "seq",
                split_axis=0,
                concat_axis=0,
                tiled=True,
            ),
            "exp",
            axis=0,
            tiled=True,
        ),
        w_gate,
        w_up,
        w_down,
    )
    whole = lax.psum_scatter(
        partial_value.astype(jnp.bfloat16), "exp", scatter_dimension=0, tiled=True
    ).astype(jnp.float32)
    returned = lax.all_to_all(
        whole.astype(jnp.bfloat16), "seq", split_axis=0, concat_axis=0, tiled=True
    ).astype(whole.dtype)
    picked = returned[pair_ids, within]
    mixture = jnp.sum((picked * shares[:, None]).reshape(-1, TOP, feature_dim), axis=1)
    return (attended, mixture.astype(jnp.bfloat16))


def solution(mesh):
    placed = (
        P(("groups", "seq"), "exp"),
        P(("groups", "seq"), "exp"),
        P(("groups", "seq"), "exp"),
        P("exp"),
        P("exp", None),
        P(("groups", "seq"), None),
        P(),
        P(("groups", "seq"), None),
        P(("groups", "seq"), None),
        P("seq", None, "exp"),
        P("seq", None, "exp"),
        P("seq", "exp", None),
    )
    return jax.shard_map(
        local,
        mesh=mesh,
        in_specs=placed,
        out_specs=(P(("groups", "seq", "exp"), None), P(("groups", "seq", "exp"), None)),
        check_vma=False,
    )
```

```python
import functools

import jax
import jax.numpy as jnp
from jax import lax
from jax.experimental import pallas as pl
from jax.experimental.pallas import tpu as pltpu
from jax.sharding import PartitionSpec as P

HEAD_DIM = 64
WINDOW = 128
TOP = 4


def shifted(value, axis, steps):
    count = lax.axis_size(axis)
    first, last = (max(0, -steps), min(count, count - steps))
    return lax.ppermute(value, axis, [(source, source + steps) for source in range(first, last)])


def swiglu(gate_val, up_val):
    return (up_val + 1.0) * gate_val * (0.5 + 0.5 * jnp.tanh(0.851 * gate_val))


def rms_norm(stream, norm_gain):
    widened = stream.astype(jnp.float32)
    spread = jnp.mean(widened * widened, axis=-1, keepdims=True)
    return (widened * lax.rsqrt(spread + 1e-05) * norm_gain).astype(jnp.bfloat16)


def window_attention(queries, key_rows, values, sink_logit):
    row_count = queries.shape[0]
    kv_local = key_rows.shape[1] // HEAD_DIM
    group_size = queries.shape[1] // HEAD_DIM // kv_local
    rim_keys, rim_values = shifted(
        (key_rows[row_count - WINDOW :], values[row_count - WINDOW :]), "seq", 1
    )
    full_keys = jnp.concatenate([rim_keys, key_rows], axis=0).reshape(
        WINDOW + row_count, kv_local, HEAD_DIM
    )
    full_values = jnp.concatenate([rim_values, values], axis=0).reshape(
        WINDOW + row_count, kv_local, HEAD_DIM
    )
    grouped = queries.reshape(row_count, kv_local, group_size, HEAD_DIM)
    scores = jnp.einsum(
        "tgjd,ugd->gjtu", grouped, full_keys, preferred_element_type=jnp.float32
    ) * HEAD_DIM ** (-0.5)
    query_pos = jnp.arange(row_count, dtype=jnp.int32)[:, None] + WINDOW
    key_pos = jnp.arange(WINDOW + row_count, dtype=jnp.int32)[None, :]
    first_key = jnp.where(lax.axis_index("seq") == 0, WINDOW, 0)
    allowed = (key_pos <= query_pos) & (key_pos > query_pos - WINDOW) & (key_pos >= first_key)
    scores = jnp.where(allowed, scores, -1e30)
    sink_vals = sink_logit.reshape(kv_local, group_size)[:, :, None, None]
    ceiling = jnp.maximum(jnp.max(scores, axis=-1, keepdims=True), sink_vals)
    raised = jnp.exp(scores - ceiling)
    denominator = jnp.sum(raised, axis=-1, keepdims=True) + jnp.exp(sink_vals - ceiling)
    weights = (raised / denominator).astype(jnp.bfloat16)
    mixed = jnp.einsum("gjtu,ugd->tgjd", weights, full_values, preferred_element_type=jnp.float32)
    return mixed.astype(jnp.bfloat16).reshape(row_count, kv_local * group_size * HEAD_DIM)


def pack_rows(normed, expert_ids, gate_codes, expert_count, capacity):
    pair_ids = expert_ids.reshape(-1)
    matches = (pair_ids[:, None] == jnp.arange(expert_count, dtype=jnp.int32)[None, :]).astype(
        jnp.float32
    )
    order = jnp.arange(pair_ids.shape[0], dtype=jnp.int32)
    earlier = (order[:, None] > order[None, :]).astype(jnp.bfloat16)
    before = jnp.dot(earlier, matches.astype(jnp.bfloat16), preferred_element_type=jnp.float32)
    within = jnp.sum(before * matches, axis=1).astype(jnp.int32)
    sources = normed[jnp.arange(pair_ids.shape[0], dtype=jnp.int32) // expert_ids.shape[1]]
    outbox = jnp.zeros((expert_count * capacity, normed.shape[1]), normed.dtype)
    outbox = outbox.at[pair_ids * capacity + within].set(sources)
    code_vals = gate_codes.astype(jnp.float32)
    shares = (code_vals / jnp.sum(code_vals, axis=1, keepdims=True)).reshape(-1)
    return (outbox, pair_ids, within, shares)


def expert_apply(arrived, w_gate, w_up, w_down):
    flat_rows = arrived.reshape(-1, arrived.shape[-1])
    gate_val = jnp.dot(flat_rows, w_gate[0], preferred_element_type=jnp.float32)
    up_val = jnp.dot(flat_rows, w_up[0], preferred_element_type=jnp.float32)
    hidden = swiglu(gate_val, up_val).astype(jnp.bfloat16)
    result = jnp.dot(hidden, w_down[0], preferred_element_type=jnp.float32)
    return result.reshape(arrived.shape)


LANES = 128
INNER = 2
CODE_ROWS = 16
PROJ_CUTS = 2
RELAY, AWAIT, APPLY, TURN, CHAIN, CROSS, FINISH = range(7)
ROW_TURNS = (0, 0, 0, 1)
PIECE_TURNS = (1, 1, 0, 0)
ORDERS = (
    (
        (RELAY, 0, 0, 2), (RELAY, 0, 0, 0), (RELAY, 0, 0, 1), (AWAIT, 0, 2), (RELAY, 0, 0, 3),
        (RELAY, 1, 0, 2), (APPLY, 0, 0), (AWAIT, 0, 0), (RELAY, 0, 1, 3), (AWAIT, 0, 1),
        (RELAY, 1, 0, 3), (RELAY, 1, 0, 1), (RELAY, 1, 0, 0), (APPLY, 1, 0), (APPLY, 0, 1),
        (AWAIT, 1, 0), (AWAIT, 1, 1), (RELAY, 2, 0, 1), (AWAIT, 1, 2), (CHAIN, 1, 0, 2, 1),
        (RELAY, 1, 1, 3), (RELAY, 2, 0, 3), (RELAY, 2, 0, 0), (APPLY, 1, 1), (RELAY, 2, 0, 2),
        (CHAIN, 1, 0, 3, 1), (AWAIT, 2, 1), (APPLY, 2, 0), (CHAIN, 1, 1, 3, 1), (RELAY, 3, 0, 2),
        (AWAIT, 2, 2), (RELAY, 2, 1, 3), (AWAIT, 2, 0), (TURN, 0, 0), (CHAIN, 2, 0, 3, 1),
        (APPLY, 2, 1), (CHAIN, 2, 0, 2, 1), (RELAY, 3, 0, 0), (CHAIN, 2, 1, 3, 1), (CHAIN, 1, 1, 2, 1),
        (RELAY, 3, 0, 3), (RELAY, 3, 0, 1), (AWAIT, 3, 2), (TURN, 0, 1), (CHAIN, 2, 1, 2, 1),
        (APPLY, 3, 0), (TURN, 2, 1), (AWAIT, 3, 0), (TURN, 1, 1), (AWAIT, 3, 1), (RELAY, 3, 1, 3),
        (CHAIN, 3, 0, 2, 1), (CHAIN, 3, 0, 3, 1), (APPLY, 3, 1), (TURN, 3, 0), (CHAIN, 3, 1, 2, 1),
        (CHAIN, 3, 1, 3, 1), (TURN, 3, 1), (CHAIN, 3, 0, 0, 1), (TURN, 2, 0), (CHAIN, 3, 0, 1, 1),
        (CHAIN, 2, 0, 1, 1), (TURN, 1, 0), (CHAIN, 2, 0, 0, 1), (CHAIN, 1, 0, 1, 1), (CROSS, 2),
        (CHAIN, 1, 0, 0, 1), (CROSS, 3), (FINISH, 0), (FINISH, 2), (FINISH, 1), (FINISH, 3),
    ),
    (
        (RELAY, 1, 0, 2), (RELAY, 1, 0, 3), (RELAY, 1, 0, 1), (RELAY, 1, 0, 0), (RELAY, 1, 1, 3),
        (RELAY, 2, 0, 3), (RELAY, 2, 0, 1), (RELAY, 0, 0, 2), (RELAY, 0, 0, 1), (RELAY, 0, 0, 3),
        (RELAY, 2, 0, 0), (RELAY, 0, 0, 0), (AWAIT, 2, 1), (AWAIT, 1, 0), (AWAIT, 1, 2),
        (RELAY, 2, 0, 2), (APPLY, 0, 0), (RELAY, 2, 1, 3), (AWAIT, 2, 0), (RELAY, 3, 0, 2),
        (APPLY, 2, 0), (RELAY, 3, 0, 0), (RELAY, 0, 1, 3), (RELAY, 3, 0, 3), (AWAIT, 0, 2),
        (APPLY, 1, 0), (AWAIT, 2, 2), (RELAY, 3, 0, 1), (APPLY, 2, 1), (AWAIT, 3, 2), (APPLY, 3, 0),
        (AWAIT, 1, 1), (AWAIT, 3, 1), (TURN, 2, 0), (RELAY, 3, 1, 3), (APPLY, 1, 1), (AWAIT, 0, 1),
        (CHAIN, 2, 0, 2, 1), (AWAIT, 3, 0), (AWAIT, 0, 0), (CHAIN, 2, 0, 3, 1), (TURN, 2, 1),
        (APPLY, 3, 1), (CHAIN, 2, 1, 3, 1), (APPLY, 0, 1), (CHAIN, 2, 1, 2, 1), (TURN, 1, 1),
        (CHAIN, 3, 0, 2, 1), (TURN, 3, 1), (TURN, 3, 0), (CHAIN, 3, 0, 3, 1), (TURN, 0, 0),
        (CHAIN, 3, 1, 2, 1), (CROSS, 2), (CHAIN, 0, 0, 2, -1), (TURN, 0, 1), (TURN, 1, 0),
        (CHAIN, 3, 1, 3, 1), (CHAIN, 0, 0, 3, -1), (CHAIN, 3, 0, 0, 1), (CHAIN, 0, 1, 2, -1),
        (CHAIN, 3, 0, 1, 1), (CHAIN, 0, 1, 3, -1), (CHAIN, 2, 0, 1, 1), (CHAIN, 0, 0, 0, -1),
        (CROSS, 3), (CHAIN, 2, 0, 0, 1), (CHAIN, 0, 0, 1, -1), (FINISH, 2), (FINISH, 3), (FINISH, 0),
        (FINISH, 1),
    ),
)


def cuts_of(extent, parts):
    edges = [extent // 16 * part // parts * 16 for part in range(parts)] + [extent]
    return [(first, last - first) for first, last in zip(edges, edges[1:])]
MESH = pl.DeviceIdType.MESH


def attend_block(me, block, sink_ref, query_buf, key_buf, value_buf, heads):
    start = block * WINDOW
    lane = lax.broadcasted_iota(jnp.int32, (2 * WINDOW, LANES), 1)
    query_pos = lax.broadcasted_iota(jnp.int32, (WINDOW, WINDOW), 0)
    key_pos = lax.broadcasted_iota(jnp.int32, (WINDOW, WINDOW), 1)
    recent = key_pos <= query_pos
    opening = (me == 0) & (block == 0)

    def halves(buf, head):
        plain = buf[start : start + 2 * WINDOW, :].astype(jnp.float32)
        turned = pltpu.roll(plain, HEAD_DIM, axis=1)
        low, high = (plain, turned) if head == 0 else (turned, plain)
        return jnp.concatenate(
            [jnp.where(lane < HEAD_DIM, low, 0.0), jnp.where(lane < HEAD_DIM, 0.0, high)], axis=0
        ).astype(jnp.bfloat16)

    pairs = query_buf.shape[1] // LANES
    for head in range(2):
        both_keys = halves(key_buf, head) * jnp.bfloat16(HEAD_DIM ** (-0.5))
        both_values = halves(value_buf, head)
        for pair in range(head * pairs // 2, (head + 1) * pairs // 2):
            columns = slice(pair * LANES, (pair + 1) * LANES)
            scores = lax.dot_general(
                query_buf[start : start + WINDOW, columns], both_keys,
                (((1,), (1,)), ((), ())), preferred_element_type=jnp.float32,
            )
            weights = []
            for half in range(2):
                sink = sink_ref[2 * pair + half]
                first = 2 * half * WINDOW
                earlier = scores[:, first : first + WINDOW]
                if block == 0:
                    earlier = jnp.where(opening, -1e30, earlier)
                seen = jnp.where(recent, scores[:, first + WINDOW : first + 2 * WINDOW], earlier)
                ceiling = jnp.maximum(jnp.max(seen, axis=1, keepdims=True), sink)
                raised = jnp.exp(seen - ceiling)
                below = jnp.sum(raised, axis=1, keepdims=True) + jnp.exp(sink - ceiling)
                shares = raised * (1.0 / below)
                weights.append(jnp.where(recent, 0.0, shares).astype(jnp.bfloat16))
                weights.append(jnp.where(recent, shares, 0.0).astype(jnp.bfloat16))
            mixed = jnp.dot(
                jnp.concatenate(weights, axis=1), both_values, preferred_element_type=jnp.float32
            )
            heads[start : start + WINDOW, columns] = mixed.astype(jnp.bfloat16)


def layer_kernel(
    sink_ref, gain_ref, routes_ref, codes_ref, query_hbm, key_hbm, value_hbm,
    o_hbm, residual_hbm, gate_hbm, up_hbm, down_hbm, attended_ref, out_ref,
    query_buf, key_buf, value_buf, o_buf, residual_buf, heads, gain_cols, stream, proj_out, proj_in,
    rim_send, rim_recv, proj_send, proj_recv, rows, part, from_core, chain_in, turn_in, cross_in,
    gate_w, up_w, down_w, gate_t, up_t, down_t,
    local_sem, row_recv, others_recv, row_send, half_send, half_recv, chain_send, chain_recv,
    turn_send, turn_recv, cross_send, cross_recv,
):
    me = lax.axis_index("seq")
    core = lax.axis_index("exp")
    other = 1 - core
    count = lax.axis_size("seq")
    outer = count // INNER
    line = me // INNER
    side = me % INNER
    has_low = jnp.minimum(line, 1)
    has_high = jnp.minimum(outer - 1 - line, 1)
    to_core = {"exp": other}
    to_pair = {"seq": line * INNER + 1 - side}
    to_high = {"seq": jnp.minimum(line + 1, outer - 1) * INNER + side}
    to_low = {"seq": jnp.maximum(line - 1, 0) * INNER + side}
    feature_dim = attended_ref.shape[0]
    flip = 2 * line // outer
    step = 1 - 2 * flip
    base = flip * (outer - 1)
    place = base + step * line
    to_ahead = {"seq": jnp.clip(line + step, 0, outer - 1) * INNER + side}
    to_back = {"seq": jnp.clip(line - step, 0, outer - 1) * INNER + side}
    row_cuts = cuts_of(rows.shape[2], len(ROW_TURNS))
    piece_cuts = cuts_of(feature_dim, len(PIECE_TURNS))
    turned_pieces = [index for index, flag in enumerate(PIECE_TURNS) if flag]
    plain_pieces = [index for index, flag in enumerate(PIECE_TURNS) if not flag]

    def chip_of(at, at_side):
        return at * INNER + at_side

    def send(src, dst, send_sem, recv_sem, where):
        return pltpu.make_async_remote_copy(
            src_ref=src, dst_ref=dst, send_sem=send_sem, recv_sem=recv_sem,
            device_id=where, device_id_type=MESH,
        )

    block_rows = proj_in.shape[1]
    row_count = query_buf.shape[0]
    has_prev = jnp.minimum(me, 1)
    has_next = jnp.minimum(count - 1 - me, 1)
    to_prev = {"seq": jnp.maximum(me - 1, 0)}
    to_next = {"seq": jnp.minimum(me + 1, count - 1)}
    own_rows = pl.ds(pl.multiple_of(core * block_rows, LANES), block_rows)
    other_rows = pl.ds(pl.multiple_of(other * block_rows, LANES), block_rows)
    inside = pl.ds(WINDOW, row_count)
    pieces = (
        (key_hbm, key_buf.at[inside]),
        (value_hbm, value_buf.at[inside]),
        (query_hbm, query_buf),
        (o_hbm, o_buf),
        (residual_hbm.at[:, own_rows], residual_buf),
        (gate_hbm.at[0], gate_w),
        (up_hbm.at[0], up_w),
        (down_hbm.at[0], down_w),
    )
    copies = [
        pltpu.make_async_copy(src, dst, local_sem.at[index])
        for index, (src, dst) in enumerate(pieces)
    ]
    for copy in copies[:5]:
        copy.start()
    barrier = pltpu.get_barrier_semaphore()
    pl.semaphore_signal(barrier, inc=1, device_id=to_core, device_id_type=MESH)
    pl.semaphore_signal(barrier, inc=1, device_id=to_pair, device_id_type=MESH)

    @pl.when(has_low == 1)
    def _():
        pl.semaphore_signal(barrier, inc=1, device_id=to_low, device_id_type=MESH)

    @pl.when(has_high == 1)
    def _():
        pl.semaphore_signal(barrier, inc=1, device_id=to_high, device_id_type=MESH)

    @pl.when(has_prev == 1)
    def _():
        pl.semaphore_signal(barrier, inc=1, device_id=to_prev, device_id_type=MESH)

    @pl.when(has_next == 1)
    def _():
        pl.semaphore_signal(barrier, inc=1, device_id=to_next, device_id_type=MESH)

    gain_cols[...] = jnp.broadcast_to(gain_ref[...].reshape(1, -1), (8, feature_dim)).T
    pl.semaphore_wait(barrier, 2 + has_low + has_high + has_prev + has_next)
    for copy in copies[:2]:
        copy.wait()

    def rim_copy(index, buf):
        return send(
            buf.at[pl.ds(row_count, WINDOW)], buf.at[pl.ds(0, WINDOW)],
            rim_send.at[index], rim_recv.at[index], to_next,
        )

    rims = (rim_copy(0, key_buf), rim_copy(1, value_buf))

    @pl.when(has_next == 1)
    def _():
        for copy in rims:
            copy.start()

    copies[2].wait()
    for copy in copies[5:]:
        copy.start()
    attend_block(me, 1, sink_ref, query_buf, key_buf, value_buf, heads)

    @pl.when(has_prev == 1)
    def _():
        for copy in rims:
            copy.wait_recv()

    @pl.when(has_prev == 0)
    def _():
        key_buf[:WINDOW] = jnp.zeros((WINDOW, key_buf.shape[1]), key_buf.dtype)
        value_buf[:WINDOW] = jnp.zeros((WINDOW, value_buf.shape[1]), value_buf.dtype)

    attend_block(me, 0, sink_ref, query_buf, key_buf, value_buf, heads)
    for copy in copies[3:5]:
        copy.wait()

    proj_cuts = cuts_of(feature_dim, proj_send.shape[0])

    def proj_copy(index):
        start, size = proj_cuts[index]
        here = pl.ds(start, size)
        return send(
            proj_out.at[here], proj_in.at[here], proj_send.at[index], proj_recv.at[index], to_core
        )

    both_heads = jnp.concatenate([heads[other_rows, :], heads[own_rows, :]], axis=0)
    for index, (start, size) in enumerate(proj_cuts):
        terms = lax.dot_general(
            o_buf[start : start + size, :], both_heads, (((1,), (1,)), ((), ())),
            preferred_element_type=jnp.float32,
        )
        proj_out[start : start + size, :] = terms[:, :block_rows].astype(jnp.bfloat16)
        proj_copy(index).start()
        stream[start : start + size, :] = (
            residual_buf[start : start + size, :].astype(jnp.float32) + terms[:, block_rows:]
        )
    own_routes = routes_ref[:, own_rows]
    own_codes = codes_ref[:, own_rows].astype(jnp.float32)
    code_rows = rows.shape[2] - feature_dim
    expert = lax.broadcasted_iota(jnp.int32, (code_rows, block_rows), 0)
    spread = jnp.zeros((code_rows, block_rows), jnp.float32)
    for choice in range(TOP):
        named = expert == own_routes[choice : choice + 1, :]
        spread = jnp.where(named, own_codes[choice : choice + 1, :], spread)
    rows[me, core, feature_dim:, :] = spread.astype(jnp.bfloat16)
    spread_sum = jnp.zeros((1, block_rows), jnp.float32)
    for index, (start, size) in enumerate(proj_cuts):
        here = slice(start, start + size)
        proj_copy(index).wait_recv()
        attended = (stream[here, :] + proj_in[here, :].astype(jnp.float32)).astype(jnp.bfloat16)
        attended_ref[here, :] = attended
        widened = attended.astype(jnp.float32)
        spread_sum = spread_sum + jnp.sum(widened * widened, axis=0, keepdims=True)
    scale = lax.rsqrt(spread_sum / feature_dim + 1e-05)
    rows[me, core, :feature_dim, :] = (
        attended_ref[...].astype(jnp.float32) * scale * gain_cols[:, :1]
    ).astype(jnp.bfloat16)

    def absolute(at):
        return base + step * at

    def block_of(at, cross):
        return chip_of(absolute(at), 1 - side if cross else side)

    def row_copy(unit, at, cross, index, kind):
        chip = block_of(at, cross)
        start, size = row_cuts[index]
        slot = rows.at[chip, core, pl.ds(start, size)]
        batch = 6 if kind == 3 else 2 * kind + (at == unit if kind == 1 else cross)
        return send(
            slot, slot, row_send.at[batch],
            others_recv.at[chip] if kind == 3 else row_recv.at[chip, index],
            (to_back, to_pair, to_ahead, to_core)[kind],
        )

    def half_copy(chip):
        return send(
            part.at[chip, other], from_core.at[chip], half_send.at[0], half_recv.at[chip], to_core
        )

    def span(index):
        start, size = piece_cuts[index]
        return pl.ds(start, size)

    def turn_copy(at, index):
        return send(
            part.at[block_of(at, 1), core, span(index)], turn_in.at[absolute(at), span(index)],
            turn_send.at[0], turn_recv.at[absolute(at), turned_pieces.index(index)], to_pair,
        )

    def chain_slot(dest, receiver, sign):
        return jnp.where((dest == receiver) & (sign * step < 0), outer, dest)

    def chain_copy(at, cross, index, sign, receiver=None):
        dest = absolute(at)
        slot = dest if receiver is None else chain_slot(dest, receiver, sign)
        column = len(PIECE_TURNS) + plain_pieces.index(index) if cross else index
        return send(
            part.at[block_of(at, cross), core, span(index)],
            chain_in.at[slot, cross, span(index)],
            chain_send.at[cross], chain_recv.at[slot, column],
            to_ahead if sign > 0 else to_back,
        )

    def cross_copy(unit, index):
        return send(
            part.at[block_of(unit, 1), core, span(index)], cross_in.at[span(index)],
            cross_send.at[0], cross_recv.at[plain_pieces.index(index)], to_pair,
        )

    def compute(chip):
        codes = jnp.concatenate(
            [rows[chip, 0, feature_dim:, :], rows[chip, 1, feature_dim:, :]], axis=1
        ).astype(jnp.float32)
        expert = lax.broadcasted_iota(jnp.int32, codes.shape, 0)
        total = jnp.sum(codes, axis=0, keepdims=True)
        mine = jnp.sum(jnp.where(expert == me, codes, 0.0), axis=0, keepdims=True)
        normed = jnp.concatenate(
            [rows[chip, 0, :feature_dim, :], rows[chip, 1, :feature_dim, :]], axis=1
        )
        parts = []
        for start, size in cuts_of(gate_t.shape[0], 5):
            here = slice(start, start + size)
            gate_val = jnp.dot(gate_t[here, :], normed, preferred_element_type=jnp.float32)
            up_val = jnp.dot(up_t[here, :], normed, preferred_element_type=jnp.float32)
            parts.append(swiglu(gate_val, up_val).astype(jnp.bfloat16))
        hidden = jnp.concatenate(parts, axis=0)
        share = mine / total
        for start, size in cuts_of(feature_dim, 3):
            here = slice(start, start + size)
            result = jnp.dot(down_t[here, :], hidden, preferred_element_type=jnp.float32)
            result = (result * share).astype(jnp.bfloat16)
            part[chip, 0, here, :] = result[:, :block_rows]
            part[chip, 1, here, :] = result[:, block_rows:]
        half_copy(chip).start()

    def add_up(dst, sources, index):
        start, size = piece_cuts[index]
        slab = next((width for width in (96, 80, 112) if size % width == 0), size)

        def one(at, carry):
            here = pl.ds(pl.multiple_of(start + at * slab, 16), slab)
            total = sources[0][here, :].astype(jnp.float32)
            for source in sources[1:]:
                total = total + source[here, :].astype(jnp.float32)
            dst[here, :] = total.astype(jnp.bfloat16)
            return carry

        lax.fori_loop(0, size // slab, one, 0)

    def sends_of(unit, task):
        kind, where = task[0], task[1:]
        if kind == RELAY:
            at, cross, index = where
            kinds = [3]
            if at <= unit < outer - 1:
                kinds.append(2)
            if at >= unit > 0:
                kinds.append(0)
            if not cross and (at == unit or not ROW_TURNS[index]):
                kinds.append(1)
            return [functools.partial(row_copy, unit, at, cross, index, way) for way in kinds[::-1]]
        if kind == AWAIT:
            at, index = where
            return [functools.partial(row_copy, unit, at, 1, index, 3)]
        if kind == TURN:
            return [functools.partial(turn_copy, *where)]
        if kind == CHAIN:
            return [functools.partial(chain_copy, *where, line + where[3] * step)]
        if kind == CROSS:
            return [functools.partial(cross_copy, unit, *where)]
        return []

    def arrivals(unit, cross, index):
        chip = block_of(unit, cross)
        sources = [part.at[chip, core], from_core.at[chip]]
        for sign, there in ((1, unit > 0), (-1, unit < outer - 1)):
            if there:
                chain_copy(unit, cross, index, sign, line).wait_recv()
                sources.append(chain_in.at[chain_slot(absolute(unit), line, sign), cross])
        return sources

    def run_task(unit, task):
        kind, where = task[0], task[1:]
        if kind == RELAY and (where[0] != unit or where[1]):
            row_copy(unit, where[0], where[1], where[2], 1).wait_recv()
        if kind == AWAIT:
            row_copy(unit, where[0], 1, where[1], 1).wait_recv()
        if kind == TURN:
            at, index = where
            chip = block_of(at, 1)
            add_up(part.at[chip, core], [part.at[chip, core], from_core.at[chip]], index)
        if kind == CHAIN:
            at, cross, index, sign = where
            chip = block_of(at, cross)
            sources = [part.at[chip, core], from_core.at[chip]]
            if PIECE_TURNS[index] and not cross:
                turn_copy(at, index).wait_recv()
                sources.append(turn_in.at[absolute(at)])
            if (unit if sign > 0 else outer - 1 - unit) > 0:
                chain_copy(at, cross, index, sign).wait_recv()
                sources.append(chain_in.at[absolute(at), cross])
            add_up(part.at[chip, core], sources, index)
        if kind == CROSS:
            sources = arrivals(unit, 1, where[0])
            add_up(part.at[block_of(unit, 1), core], sources, where[0])
        if kind == FINISH:
            index = where[0]
            sources = arrivals(unit, 0, index)
            if PIECE_TURNS[index]:
                turn_copy(unit, index).wait_recv()
                sources.append(turn_in.at[absolute(unit)])
            else:
                cross_copy(unit, index).wait_recv()
                sources.append(cross_in)
            add_up(out_ref, sources, index)
        for make in sends_of(unit, task):
            make().start()

    def all_sent(buf, blocks, extent, sem):
        if blocks * extent:
            sent = buf.at[pl.ds(0, blocks), core, pl.ds(0, extent)]
            pltpu.make_async_copy(sent, sent, sem).wait()

    def plan_of(unit):
        stretches, blocks, seen = [[]], [], set()
        for task in ORDERS[unit]:
            if task[0] == APPLY:
                blocks.append(task[1:])
                stretches.append([])
                continue
            need = {
                TURN: lambda: (task[1], 1),
                CHAIN: lambda: (task[1], task[2]),
                CROSS: lambda: (unit, 1),
                FINISH: lambda: (unit, 0),
            }.get(task[0], lambda: None)()
            fresh = need is not None and need not in seen
            seen.add(need)
            stretches[-1].append((task, need if fresh else None))
        return stretches, blocks

    plans = [plan_of(unit) for unit in range(len(ORDERS))]

    def run_stretch(unit, stretch):
        for task, fresh in stretch:
            if fresh is not None:
                half_copy(block_of(*fresh)).wait_recv()
            run_task(unit, task)

    def one_block(turn, carry):
        at = jnp.int32(0)
        cross = jnp.int32(0)
        for unit, (stretches, blocks) in enumerate(plans):
            for number, (block_at, block_cross) in enumerate(blocks):
                here = (place == unit) & (turn == number)
                at = jnp.where(here, block_at, at)
                cross = jnp.where(here, block_cross, cross)

                @pl.when(here)
                def _(unit=unit, stretch=stretches[number]):
                    run_stretch(unit, stretch)

        @pl.when(turn == 0)
        def _():
            for copy in copies[5:]:
                copy.wait()
            gate_t[...] = gate_w[...].T
            up_t[...] = up_w[...].T
            down_t[...] = down_w[...].T

        chip = chip_of(absolute(at), side + cross * (1 - 2 * side))
        slot = rows.at[chip, other]
        send(slot, slot, row_send.at[6], others_recv.at[chip], to_core).wait_recv()
        compute(chip)
        return carry

    lax.fori_loop(0, count, one_block, 0)
    for unit, (stretches, blocks) in enumerate(plans):
        @pl.when(place == unit)
        def _(unit=unit, stretches=stretches):
            run_stretch(unit, stretches[-1])
            turned_rows = sum(row_cuts[index][1] for index, flag in enumerate(ROW_TURNS) if flag)
            for kind, blocks in ((0, outer - unit if unit else 0), (2, unit + 1)):
                all_sent(rows, blocks, rows.shape[2], row_send.at[2 * kind])
                all_sent(rows, blocks, turned_rows, row_send.at[2 * kind + 1])
            all_sent(rows, 1, rows.shape[2], row_send.at[3])
            all_sent(rows, outer - 1, rows.shape[2] - turned_rows, row_send.at[2])

    first_rows = sum(piece_cuts[index][1] for index in turned_pieces)
    all_sent(rows, count, rows.shape[2], row_send.at[6])
    all_sent(part, count, feature_dim, half_send.at[0])
    all_sent(part, outer, first_rows, turn_send.at[0])
    all_sent(part, 1, feature_dim - first_rows, cross_send.at[0])
    all_sent(part, outer - 1, feature_dim, chain_send.at[0])
    all_sent(part, outer - 1, feature_dim - first_rows, chain_send.at[1])
    for index in range(len(proj_cuts)):
        proj_copy(index).wait_send()

    @pl.when(has_next == 1)
    def _():
        for copy in rims:
            copy.wait_send()


def hand_on(attended_ref, mixture_ref, attended_out, mixture_out, went):
    copies = [
        pltpu.make_async_copy(attended_ref, attended_out, went.at[0]),
        pltpu.make_async_copy(mixture_ref, mixture_out, went.at[1]),
    ]
    for copy in copies:
        copy.start()
    for copy in copies:
        copy.wait()


def whole_layer(
    queries, key_rows, values, sink_logit, o_weight, residual, norm_gain, routes, gate_codes,
    w_gate, w_up, w_down,
):
    row_count, feature_dim = residual.shape
    block_rows = row_count // 2
    chips = lax.axis_size("seq")
    outer = chips // INNER
    hidden_dim = w_gate.shape[2]
    turned = (feature_dim, block_rows)
    coded = (feature_dim + CODE_ROWS, block_rows)
    chunks, pieces = len(ROW_TURNS), len(PIECE_TURNS)
    dma = pltpu.SemaphoreType.DMA
    vmem = pl.BlockSpec(memory_space=pltpu.VMEM)
    half = jnp.bfloat16
    attended, mixture = pl.pallas_call(
        layer_kernel,
        out_shape=(pltpu.VMEM(turned, half), pltpu.VMEM(turned, half)),
        in_specs=[pl.BlockSpec(memory_space=pltpu.SMEM), vmem, vmem, vmem]
        + [pl.BlockSpec(memory_space=pl.ANY)] * 8,
        out_specs=(vmem, vmem),
        scratch_shapes=[
            pltpu.VMEM(queries.shape, half),
            pltpu.VMEM((WINDOW + row_count, key_rows.shape[1]), half),
            pltpu.VMEM((WINDOW + row_count, values.shape[1]), half),
            pltpu.VMEM(o_weight.shape[::-1], half),
            pltpu.VMEM(turned, half),
            pltpu.VMEM(queries.shape, half),
            pltpu.VMEM((feature_dim, 8), jnp.float32),
            pltpu.VMEM(turned, jnp.float32),
            pltpu.VMEM(turned, half),
            pltpu.VMEM(turned, half),
            dma((2,)),
            dma((2,)),
            dma((PROJ_CUTS,)),
            dma((PROJ_CUTS,)),
            pltpu.VMEM((chips, 2) + coded, half),
            pltpu.VMEM((chips, 2) + turned, half),
            pltpu.VMEM((chips,) + turned, half),
            pltpu.VMEM((outer + 1, 2) + turned, half),
            pltpu.VMEM((outer,) + turned, half),
            pltpu.VMEM(turned, half),
            pltpu.VMEM((feature_dim, hidden_dim), half),
            pltpu.VMEM((feature_dim, hidden_dim), half),
            pltpu.VMEM((hidden_dim, feature_dim), half),
            pltpu.VMEM((hidden_dim, feature_dim), half),
            pltpu.VMEM((hidden_dim, feature_dim), half),
            pltpu.VMEM((feature_dim, hidden_dim), half),
            dma((8,)),
            dma((chips, chunks)),
            dma((chips,)),
            dma((7,)),
            dma((1,)),
            dma((chips,)),
            dma((2,)),
            dma((outer + 1, 2 * pieces - sum(PIECE_TURNS))),
            dma((1,)),
            dma((outer, sum(PIECE_TURNS))),
            dma((1,)),
            dma((pieces - sum(PIECE_TURNS),)),
        ],
        compiler_params=pltpu.CompilerParams(
            collective_id=1, has_side_effects=True, vmem_limit_bytes=60 << 20
        ),
    )(
        sink_logit, norm_gain, routes.T, gate_codes.T, queries, key_rows, values,
        o_weight.T, residual.T, w_gate, w_up, w_down,
    )
    attended, mixture = pl.pallas_call(
        hand_on,
        out_shape=(jax.ShapeDtypeStruct(turned, half), jax.ShapeDtypeStruct(turned, half)),
        in_specs=[vmem] * 2,
        out_specs=(pl.BlockSpec(memory_space=pl.ANY),) * 2,
        scratch_shapes=[dma((2,))],
    )(*(pltpu.with_memory_space_constraint(value, pltpu.VMEM) for value in (attended, mixture)))
    return (attended.T, mixture.T)


def fits_kernel(queries, key_rows, residual, w_gate):
    chips = lax.axis_size("seq")
    return (
        lax.axis_size("exp") == 2
        and chips % INNER == 0
        and chips <= CODE_ROWS
        and residual.shape[1] % 16 == 0
        and chips == 2 * INNER * len(ORDERS)
        and w_gate.shape[0] == 1
        and residual.shape[0] == 2 * WINDOW
        and 2 * TOP >= chips
        and key_rows.shape[1] == LANES
        and queries.shape[1] % (2 * LANES) == 0
    )


def local(
    queries,
    key_rows,
    values,
    sink_logit,
    o_weight,
    residual,
    norm_gain,
    routes,
    gate_codes,
    w_gate,
    w_up,
    w_down,
):
    if fits_kernel(queries, key_rows, residual, w_gate):
        return whole_layer(
            queries, key_rows, values, sink_logit, o_weight, residual, norm_gain, routes,
            gate_codes, w_gate, w_up, w_down,
        )
    heads_out = window_attention(queries, key_rows, values, sink_logit)
    proj_terms = jnp.dot(heads_out, o_weight, preferred_element_type=jnp.float32)
    owners = lax.axis_size("exp")
    owner_pos = lax.axis_index("exp")
    block_rows = residual.shape[0] // owners
    expert_count = w_gate.shape[0] * lax.axis_size("seq")
    capacity = max(2, 2 * block_rows * TOP // expert_count)
    feature_dim = residual.shape[1]
    own_stream = lax.dynamic_slice_in_dim(residual, owner_pos * block_rows, block_rows, 0)
    own_routes = lax.dynamic_slice_in_dim(routes, owner_pos * block_rows, block_rows, 0)
    own_codes = lax.dynamic_slice_in_dim(gate_codes, owner_pos * block_rows, block_rows, 0)
    own_terms = lax.psum_scatter(proj_terms, "exp", scatter_dimension=0, tiled=True)
    attended = (own_stream.astype(jnp.float32) + own_terms).astype(jnp.bfloat16)
    normed = rms_norm(attended, norm_gain)
    outbox, pair_ids, within, shares = pack_rows(
        normed, own_routes, own_codes, expert_count, capacity
    )
    partial_value = expert_apply(
        lax.all_gather(
            lax.all_to_all(
                outbox.reshape(expert_count, capacity, feature_dim),
                "seq",
                split_axis=0,
                concat_axis=0,
                tiled=True,
            ),
            "exp",
            axis=0,
            tiled=True,
        ),
        w_gate,
        w_up,
        w_down,
    )
    whole = lax.psum_scatter(
        partial_value.astype(jnp.bfloat16), "exp", scatter_dimension=0, tiled=True
    ).astype(jnp.float32)
    returned = lax.all_to_all(
        whole.astype(jnp.bfloat16), "seq", split_axis=0, concat_axis=0, tiled=True
    ).astype(whole.dtype)
    picked = returned[pair_ids, within]
    mixture = jnp.sum((picked * shares[:, None]).reshape(-1, TOP, feature_dim), axis=1)
    return (attended, mixture.astype(jnp.bfloat16))


def solution(mesh):
    placed = (
        P(("groups", "seq"), "exp"),
        P(("groups", "seq"), "exp"),
        P(("groups", "seq"), "exp"),
        P("exp"),
        P("exp", None),
        P(("groups", "seq"), None),
        P(),
        P(("groups", "seq"), None),
        P(("groups", "seq"), None),
        P("seq", None, "exp"),
        P("seq", None, "exp"),
        P("seq", "exp", None),
    )
    return jax.shard_map(
        local,
        mesh=mesh,
        in_specs=placed,
        out_specs=(P(("groups", "seq", "exp"), None), P(("groups", "seq", "exp"), None)),
        check_vma=False,
    )
```

```python
import functools

import jax
import jax.numpy as jnp
from jax import lax
from jax.experimental import pallas as pl
from jax.experimental.pallas import tpu as pltpu
from jax.sharding import PartitionSpec as P

HEAD_DIM = 64
WINDOW = 128
TOP = 4


def shifted(value, axis, steps):
    count = lax.axis_size(axis)
    first, last = (max(0, -steps), min(count, count - steps))
    return lax.ppermute(value, axis, [(source, source + steps) for source in range(first, last)])


def swiglu(gate_val, up_val):
    return (up_val + 1.0) * gate_val * (0.5 + 0.5 * jnp.tanh(0.851 * gate_val))


def rms_norm(stream, norm_gain):
    widened = stream.astype(jnp.float32)
    spread = jnp.mean(widened * widened, axis=-1, keepdims=True)
    return (widened * lax.rsqrt(spread + 1e-05) * norm_gain).astype(jnp.bfloat16)


def window_attention(queries, key_rows, values, sink_logit):
    row_count = queries.shape[0]
    kv_local = key_rows.shape[1] // HEAD_DIM
    group_size = queries.shape[1] // HEAD_DIM // kv_local
    rim_keys, rim_values = shifted(
        (key_rows[row_count - WINDOW :], values[row_count - WINDOW :]), "seq", 1
    )
    full_keys = jnp.concatenate([rim_keys, key_rows], axis=0).reshape(
        WINDOW + row_count, kv_local, HEAD_DIM
    )
    full_values = jnp.concatenate([rim_values, values], axis=0).reshape(
        WINDOW + row_count, kv_local, HEAD_DIM
    )
    grouped = queries.reshape(row_count, kv_local, group_size, HEAD_DIM)
    scores = jnp.einsum(
        "tgjd,ugd->gjtu", grouped, full_keys, preferred_element_type=jnp.float32
    ) * HEAD_DIM ** (-0.5)
    query_pos = jnp.arange(row_count, dtype=jnp.int32)[:, None] + WINDOW
    key_pos = jnp.arange(WINDOW + row_count, dtype=jnp.int32)[None, :]
    first_key = jnp.where(lax.axis_index("seq") == 0, WINDOW, 0)
    allowed = (key_pos <= query_pos) & (key_pos > query_pos - WINDOW) & (key_pos >= first_key)
    scores = jnp.where(allowed, scores, -1e30)
    sink_vals = sink_logit.reshape(kv_local, group_size)[:, :, None, None]
    ceiling = jnp.maximum(jnp.max(scores, axis=-1, keepdims=True), sink_vals)
    raised = jnp.exp(scores - ceiling)
    denominator = jnp.sum(raised, axis=-1, keepdims=True) + jnp.exp(sink_vals - ceiling)
    weights = (raised / denominator).astype(jnp.bfloat16)
    mixed = jnp.einsum("gjtu,ugd->tgjd", weights, full_values, preferred_element_type=jnp.float32)
    return mixed.astype(jnp.bfloat16).reshape(row_count, kv_local * group_size * HEAD_DIM)


def pack_rows(normed, expert_ids, gate_codes, expert_count, capacity):
    pair_ids = expert_ids.reshape(-1)
    matches = (pair_ids[:, None] == jnp.arange(expert_count, dtype=jnp.int32)[None, :]).astype(
        jnp.float32
    )
    order = jnp.arange(pair_ids.shape[0], dtype=jnp.int32)
    earlier = (order[:, None] > order[None, :]).astype(jnp.bfloat16)
    before = jnp.dot(earlier, matches.astype(jnp.bfloat16), preferred_element_type=jnp.float32)
    within = jnp.sum(before * matches, axis=1).astype(jnp.int32)
    sources = normed[jnp.arange(pair_ids.shape[0], dtype=jnp.int32) // expert_ids.shape[1]]
    outbox = jnp.zeros((expert_count * capacity, normed.shape[1]), normed.dtype)
    outbox = outbox.at[pair_ids * capacity + within].set(sources)
    code_vals = gate_codes.astype(jnp.float32)
    shares = (code_vals / jnp.sum(code_vals, axis=1, keepdims=True)).reshape(-1)
    return (outbox, pair_ids, within, shares)


def expert_apply(arrived, w_gate, w_up, w_down):
    flat_rows = arrived.reshape(-1, arrived.shape[-1])
    gate_val = jnp.dot(flat_rows, w_gate[0], preferred_element_type=jnp.float32)
    up_val = jnp.dot(flat_rows, w_up[0], preferred_element_type=jnp.float32)
    hidden = swiglu(gate_val, up_val).astype(jnp.bfloat16)
    result = jnp.dot(hidden, w_down[0], preferred_element_type=jnp.float32)
    return result.reshape(arrived.shape)


LANES = 128
INNER = 2
CODE_ROWS = 16
PROJ_CUTS = 2
RELAY, AWAIT, APPLY, TURN, CHAIN, CROSS, FINISH = range(7)
ROW_TURNS = (0, 0, 0, 1)
PIECE_TURNS = (1, 1, 0, 0)
ORDERS = (
    (
        (RELAY, 0, 0, 2), (RELAY, 0, 0, 0), (RELAY, 0, 0, 1), (AWAIT, 0, 2), (RELAY, 0, 0, 3),
        (RELAY, 1, 0, 2), (APPLY, 0, 0), (AWAIT, 0, 0), (RELAY, 0, 1, 3), (AWAIT, 0, 1),
        (RELAY, 1, 0, 3), (RELAY, 1, 0, 1), (RELAY, 1, 0, 0), (APPLY, 1, 0), (APPLY, 0, 1),
        (AWAIT, 1, 0), (AWAIT, 1, 1), (RELAY, 2, 0, 1), (AWAIT, 1, 2), (CHAIN, 1, 0, 2, 1),
        (RELAY, 1, 1, 3), (RELAY, 2, 0, 3), (RELAY, 2, 0, 0), (APPLY, 1, 1), (RELAY, 2, 0, 2),
        (CHAIN, 1, 0, 3, 1), (AWAIT, 2, 1), (APPLY, 2, 0), (CHAIN, 1, 1, 3, 1), (RELAY, 3, 0, 2),
        (AWAIT, 2, 2), (RELAY, 2, 1, 3), (AWAIT, 2, 0), (TURN, 0, 0), (CHAIN, 2, 0, 3, 1),
        (APPLY, 2, 1), (CHAIN, 2, 0, 2, 1), (RELAY, 3, 0, 0), (CHAIN, 2, 1, 3, 1), (CHAIN, 1, 1, 2, 1),
        (RELAY, 3, 0, 3), (RELAY, 3, 0, 1), (AWAIT, 3, 2), (TURN, 0, 1), (CHAIN, 2, 1, 2, 1),
        (APPLY, 3, 0), (TURN, 2, 1), (AWAIT, 3, 0), (TURN, 1, 1), (AWAIT, 3, 1), (RELAY, 3, 1, 3),
        (CHAIN, 3, 0, 2, 1), (CHAIN, 3, 0, 3, 1), (APPLY, 3, 1), (TURN, 3, 0), (CHAIN, 3, 1, 2, 1),
        (CHAIN, 3, 1, 3, 1), (TURN, 3, 1), (CHAIN, 3, 0, 0, 1), (TURN, 2, 0), (CHAIN, 3, 0, 1, 1),
        (CHAIN, 2, 0, 1, 1), (TURN, 1, 0), (CHAIN, 2, 0, 0, 1), (CHAIN, 1, 0, 1, 1), (CROSS, 2),
        (CHAIN, 1, 0, 0, 1), (CROSS, 3), (FINISH, 0), (FINISH, 2), (FINISH, 1), (FINISH, 3),
    ),
    (
        (RELAY, 1, 0, 2), (RELAY, 1, 0, 3), (RELAY, 1, 0, 1), (RELAY, 1, 0, 0), (RELAY, 1, 1, 3),
        (RELAY, 2, 0, 3), (RELAY, 2, 0, 1), (RELAY, 0, 0, 2), (RELAY, 0, 0, 1), (RELAY, 0, 0, 3),
        (RELAY, 2, 0, 0), (RELAY, 0, 0, 0), (AWAIT, 2, 1), (AWAIT, 1, 0), (AWAIT, 1, 2),
        (RELAY, 2, 0, 2), (APPLY, 0, 0), (RELAY, 2, 1, 3), (AWAIT, 2, 0), (RELAY, 3, 0, 2),
        (APPLY, 2, 0), (RELAY, 3, 0, 0), (RELAY, 0, 1, 3), (RELAY, 3, 0, 3), (AWAIT, 0, 2),
        (APPLY, 1, 0), (AWAIT, 2, 2), (RELAY, 3, 0, 1), (APPLY, 2, 1), (AWAIT, 3, 2), (APPLY, 3, 0),
        (AWAIT, 1, 1), (AWAIT, 3, 1), (TURN, 2, 0), (RELAY, 3, 1, 3), (APPLY, 1, 1), (AWAIT, 0, 1),
        (CHAIN, 2, 0, 2, 1), (AWAIT, 3, 0), (AWAIT, 0, 0), (CHAIN, 2, 0, 3, 1), (TURN, 2, 1),
        (APPLY, 3, 1), (CHAIN, 2, 1, 3, 1), (APPLY, 0, 1), (CHAIN, 2, 1, 2, 1), (TURN, 1, 1),
        (CHAIN, 3, 0, 2, 1), (TURN, 3, 1), (TURN, 3, 0), (CHAIN, 3, 0, 3, 1), (TURN, 0, 0),
        (CHAIN, 3, 1, 2, 1), (CROSS, 2), (CHAIN, 0, 0, 2, -1), (TURN, 0, 1), (TURN, 1, 0),
        (CHAIN, 3, 1, 3, 1), (CHAIN, 0, 0, 3, -1), (CHAIN, 3, 0, 0, 1), (CHAIN, 0, 1, 2, -1),
        (CHAIN, 3, 0, 1, 1), (CHAIN, 0, 1, 3, -1), (CHAIN, 2, 0, 1, 1), (CHAIN, 0, 0, 0, -1),
        (CROSS, 3), (CHAIN, 2, 0, 0, 1), (CHAIN, 0, 0, 1, -1), (FINISH, 2), (FINISH, 3), (FINISH, 0),
        (FINISH, 1),
    ),
)


def cuts_of(extent, parts):
    edges = [extent // 16 * part // parts * 16 for part in range(parts)] + [extent]
    return [(first, last - first) for first, last in zip(edges, edges[1:])]
MESH = pl.DeviceIdType.MESH


def attend_block(me, block, sink_ref, query_buf, key_buf, value_buf, heads):
    start = block * WINDOW
    lane = lax.broadcasted_iota(jnp.int32, (2 * WINDOW, LANES), 1)
    query_pos = lax.broadcasted_iota(jnp.int32, (WINDOW, WINDOW), 0)
    key_pos = lax.broadcasted_iota(jnp.int32, (WINDOW, WINDOW), 1)
    recent = key_pos <= query_pos
    opening = (me == 0) & (block == 0)

    def halves(buf, head):
        plain = buf[start : start + 2 * WINDOW, :].astype(jnp.float32)
        turned = pltpu.roll(plain, HEAD_DIM, axis=1)
        low, high = (plain, turned) if head == 0 else (turned, plain)
        return jnp.concatenate(
            [jnp.where(lane < HEAD_DIM, low, 0.0), jnp.where(lane < HEAD_DIM, 0.0, high)], axis=0
        ).astype(jnp.bfloat16)

    pairs = query_buf.shape[1] // LANES
    for head in range(2):
        both_keys = halves(key_buf, head) * jnp.bfloat16(HEAD_DIM ** (-0.5))
        both_values = halves(value_buf, head)
        for pair in range(head * pairs // 2, (head + 1) * pairs // 2):
            columns = slice(pair * LANES, (pair + 1) * LANES)
            scores = lax.dot_general(
                query_buf[start : start + WINDOW, columns], both_keys,
                (((1,), (1,)), ((), ())), preferred_element_type=jnp.float32,
            )
            weights = []
            for half in range(2):
                sink = sink_ref[2 * pair + half]
                first = 2 * half * WINDOW
                earlier = scores[:, first : first + WINDOW]
                if block == 0:
                    earlier = jnp.where(opening, -1e30, earlier)
                seen = jnp.where(recent, scores[:, first + WINDOW : first + 2 * WINDOW], earlier)
                ceiling = jnp.maximum(jnp.max(seen, axis=1, keepdims=True), sink)
                raised = jnp.exp(seen - ceiling)
                below = jnp.sum(raised, axis=1, keepdims=True) + jnp.exp(sink - ceiling)
                shares = raised * (1.0 / below)
                weights.append(jnp.where(recent, 0.0, shares).astype(jnp.bfloat16))
                weights.append(jnp.where(recent, shares, 0.0).astype(jnp.bfloat16))
            mixed = jnp.dot(
                jnp.concatenate(weights, axis=1), both_values, preferred_element_type=jnp.float32
            )
            heads[start : start + WINDOW, columns] = mixed.astype(jnp.bfloat16)


def layer_kernel(
    sink_ref, gain_ref, routes_ref, codes_ref, query_hbm, key_hbm, value_hbm,
    o_hbm, residual_hbm, gate_hbm, up_hbm, down_hbm, attended_ref, out_ref,
    query_buf, key_buf, value_buf, o_buf, residual_buf, heads, gain_cols, stream, proj_out, proj_in,
    rim_send, rim_recv, proj_send, proj_recv, rows, part, from_core, chain_in, turn_in, cross_in,
    gate_w, up_w, down_w, gate_t, up_t, down_t,
    local_sem, row_recv, others_recv, row_send, half_send, half_recv, chain_send, chain_recv,
    turn_send, turn_recv, cross_send, cross_recv,
):
    me = lax.axis_index("seq")
    core = lax.axis_index("exp")
    other = 1 - core
    count = lax.axis_size("seq")
    outer = count // INNER
    line = me // INNER
    side = me % INNER
    has_low = jnp.minimum(line, 1)
    has_high = jnp.minimum(outer - 1 - line, 1)
    to_core = {"exp": other}
    to_pair = {"seq": line * INNER + 1 - side}
    to_high = {"seq": jnp.minimum(line + 1, outer - 1) * INNER + side}
    to_low = {"seq": jnp.maximum(line - 1, 0) * INNER + side}
    feature_dim = attended_ref.shape[0]
    flip = 2 * line // outer
    step = 1 - 2 * flip
    base = flip * (outer - 1)
    place = base + step * line
    to_ahead = {"seq": jnp.clip(line + step, 0, outer - 1) * INNER + side}
    to_back = {"seq": jnp.clip(line - step, 0, outer - 1) * INNER + side}
    row_cuts = cuts_of(rows.shape[2], len(ROW_TURNS))
    piece_cuts = cuts_of(feature_dim, len(PIECE_TURNS))
    turned_pieces = [index for index, flag in enumerate(PIECE_TURNS) if flag]
    plain_pieces = [index for index, flag in enumerate(PIECE_TURNS) if not flag]

    def chip_of(at, at_side):
        return at * INNER + at_side

    def send(src, dst, send_sem, recv_sem, where):
        return pltpu.make_async_remote_copy(
            src_ref=src, dst_ref=dst, send_sem=send_sem, recv_sem=recv_sem,
            device_id=where, device_id_type=MESH,
        )

    block_rows = proj_in.shape[1]
    row_count = query_buf.shape[0]
    has_prev = jnp.minimum(me, 1)
    has_next = jnp.minimum(count - 1 - me, 1)
    to_prev = {"seq": jnp.maximum(me - 1, 0)}
    to_next = {"seq": jnp.minimum(me + 1, count - 1)}
    own_rows = pl.ds(pl.multiple_of(core * block_rows, LANES), block_rows)
    other_rows = pl.ds(pl.multiple_of(other * block_rows, LANES), block_rows)
    inside = pl.ds(WINDOW, row_count)
    pieces = (
        (key_hbm, key_buf.at[inside]),
        (value_hbm, value_buf.at[inside]),
        (query_hbm, query_buf),
        (o_hbm, o_buf),
        (residual_hbm.at[:, own_rows], residual_buf),
        (gate_hbm.at[0], gate_w),
        (up_hbm.at[0], up_w),
        (down_hbm.at[0], down_w),
    )
    copies = [
        pltpu.make_async_copy(src, dst, local_sem.at[index])
        for index, (src, dst) in enumerate(pieces)
    ]
    for copy in copies[:5]:
        copy.start()
    barrier = pltpu.get_barrier_semaphore()
    pl.semaphore_signal(barrier, inc=1, device_id=to_core, device_id_type=MESH)
    pl.semaphore_signal(barrier, inc=1, device_id=to_pair, device_id_type=MESH)

    @pl.when(has_low == 1)
    def _():
        pl.semaphore_signal(barrier, inc=1, device_id=to_low, device_id_type=MESH)

    @pl.when(has_high == 1)
    def _():
        pl.semaphore_signal(barrier, inc=1, device_id=to_high, device_id_type=MESH)

    @pl.when(has_prev == 1)
    def _():
        pl.semaphore_signal(barrier, inc=1, device_id=to_prev, device_id_type=MESH)

    @pl.when(has_next == 1)
    def _():
        pl.semaphore_signal(barrier, inc=1, device_id=to_next, device_id_type=MESH)

    gain_cols[...] = jnp.broadcast_to(
        gain_ref[...].reshape(1, -1), (block_rows, feature_dim)
    ).T
    pl.semaphore_wait(barrier, 2 + has_low + has_high + has_prev + has_next)
    for copy in copies[:2]:
        copy.wait()

    def rim_copy(index, buf):
        return send(
            buf.at[pl.ds(row_count, WINDOW)], buf.at[pl.ds(0, WINDOW)],
            rim_send.at[index], rim_recv.at[index], to_next,
        )

    rims = (rim_copy(0, key_buf), rim_copy(1, value_buf))

    @pl.when(has_next == 1)
    def _():
        for copy in rims:
            copy.start()

    copies[2].wait()
    for copy in copies[5:]:
        copy.start()
    attend_block(me, 1, sink_ref, query_buf, key_buf, value_buf, heads)

    @pl.when(has_prev == 1)
    def _():
        for copy in rims:
            copy.wait_recv()

    @pl.when(has_prev == 0)
    def _():
        key_buf[:WINDOW] = jnp.zeros((WINDOW, key_buf.shape[1]), key_buf.dtype)
        value_buf[:WINDOW] = jnp.zeros((WINDOW, value_buf.shape[1]), value_buf.dtype)

    attend_block(me, 0, sink_ref, query_buf, key_buf, value_buf, heads)
    for copy in copies[3:5]:
        copy.wait()

    proj_cuts = cuts_of(feature_dim, proj_send.shape[0])

    def proj_copy(index):
        start, size = proj_cuts[index]
        here = pl.ds(start, size)
        return send(
            proj_out.at[here], proj_in.at[here], proj_send.at[index], proj_recv.at[index], to_core
        )

    both_heads = jnp.concatenate([heads[other_rows, :], heads[own_rows, :]], axis=0)
    for index, (start, size) in enumerate(proj_cuts):
        terms = lax.dot_general(
            o_buf[start : start + size, :], both_heads, (((1,), (1,)), ((), ())),
            preferred_element_type=jnp.float32,
        )
        proj_out[start : start + size, :] = terms[:, :block_rows].astype(jnp.bfloat16)
        proj_copy(index).start()
        stream[start : start + size, :] = (
            residual_buf[start : start + size, :].astype(jnp.float32) + terms[:, block_rows:]
        )
    own_routes = routes_ref[:, own_rows]
    own_codes = codes_ref[:, own_rows].astype(jnp.float32)
    code_rows = rows.shape[2] - feature_dim
    expert = lax.broadcasted_iota(jnp.int32, (code_rows, block_rows), 0)
    spread = jnp.zeros((code_rows, block_rows), jnp.float32)
    for choice in range(TOP):
        named = expert == own_routes[choice : choice + 1, :]
        spread = jnp.where(named, own_codes[choice : choice + 1, :], spread)
    rows[me, core, feature_dim:, :] = spread.astype(jnp.bfloat16)
    spread_sum = jnp.zeros((1, block_rows), jnp.float32)
    for index, (start, size) in enumerate(proj_cuts):
        here = slice(start, start + size)
        proj_copy(index).wait_recv()
        attended = (stream[here, :] + proj_in[here, :].astype(jnp.float32)).astype(jnp.bfloat16)
        attended_ref[here, :] = attended
        widened = attended.astype(jnp.float32)
        spread_sum = spread_sum + jnp.sum(widened * widened, axis=0, keepdims=True)
    scale = lax.rsqrt(spread_sum / feature_dim + 1e-05)
    rows[me, core, :feature_dim, :] = (
        attended_ref[...].astype(jnp.float32) * scale * gain_cols[...]
    ).astype(jnp.bfloat16)

    def absolute(at):
        return base + step * at

    def block_of(at, cross):
        return chip_of(absolute(at), 1 - side if cross else side)

    def row_copy(unit, at, cross, index, kind):
        chip = block_of(at, cross)
        start, size = row_cuts[index]
        slot = rows.at[chip, core, pl.ds(start, size)]
        batch = 6 if kind == 3 else 2 * kind + (at == unit if kind == 1 else cross)
        return send(
            slot, slot, row_send.at[batch],
            others_recv.at[chip] if kind == 3 else row_recv.at[chip, index],
            (to_back, to_pair, to_ahead, to_core)[kind],
        )

    def half_copy(chip):
        return send(
            part.at[chip, other], from_core.at[chip], half_send.at[0], half_recv.at[chip], to_core
        )

    def span(index):
        start, size = piece_cuts[index]
        return pl.ds(start, size)

    def turn_copy(at, index):
        return send(
            part.at[block_of(at, 1), core, span(index)], turn_in.at[absolute(at), span(index)],
            turn_send.at[0], turn_recv.at[absolute(at), turned_pieces.index(index)], to_pair,
        )

    def chain_slot(dest, receiver, sign):
        return jnp.where((dest == receiver) & (sign * step < 0), outer, dest)

    def chain_copy(at, cross, index, sign, receiver=None):
        dest = absolute(at)
        slot = dest if receiver is None else chain_slot(dest, receiver, sign)
        column = len(PIECE_TURNS) + plain_pieces.index(index) if cross else index
        return send(
            part.at[block_of(at, cross), core, span(index)],
            chain_in.at[slot, cross, span(index)],
            chain_send.at[cross], chain_recv.at[slot, column],
            to_ahead if sign > 0 else to_back,
        )

    def cross_copy(unit, index):
        return send(
            part.at[block_of(unit, 1), core, span(index)], cross_in.at[span(index)],
            cross_send.at[0], cross_recv.at[plain_pieces.index(index)], to_pair,
        )

    def compute(chip):
        codes = jnp.concatenate(
            [rows[chip, 0, feature_dim:, :], rows[chip, 1, feature_dim:, :]], axis=1
        ).astype(jnp.float32)
        expert = lax.broadcasted_iota(jnp.int32, codes.shape, 0)
        total = jnp.sum(codes, axis=0, keepdims=True)
        mine = jnp.sum(jnp.where(expert == me, codes, 0.0), axis=0, keepdims=True)
        normed = jnp.concatenate(
            [rows[chip, 0, :feature_dim, :], rows[chip, 1, :feature_dim, :]], axis=1
        )
        parts = []
        for start, size in cuts_of(gate_t.shape[0], 5):
            here = slice(start, start + size)
            gate_val = jnp.dot(gate_t[here, :], normed, preferred_element_type=jnp.float32)
            up_val = jnp.dot(up_t[here, :], normed, preferred_element_type=jnp.float32)
            parts.append(swiglu(gate_val, up_val).astype(jnp.bfloat16))
        hidden = jnp.concatenate(parts, axis=0)
        share = mine / total
        for start, size in cuts_of(feature_dim, 3):
            here = slice(start, start + size)
            result = jnp.dot(down_t[here, :], hidden, preferred_element_type=jnp.float32)
            result = (result * share).astype(jnp.bfloat16)
            part[chip, 0, here, :] = result[:, :block_rows]
            part[chip, 1, here, :] = result[:, block_rows:]
        half_copy(chip).start()

    def add_up(dst, sources, index):
        start, size = piece_cuts[index]
        slab = next((width for width in (96, 80, 112) if size % width == 0), size)

        def one(at, carry):
            here = pl.ds(pl.multiple_of(start + at * slab, 16), slab)
            total = sources[0][here, :].astype(jnp.float32)
            for source in sources[1:]:
                total = total + source[here, :].astype(jnp.float32)
            dst[here, :] = total.astype(jnp.bfloat16)
            return carry

        lax.fori_loop(0, size // slab, one, 0)

    def sends_of(unit, task):
        kind, where = task[0], task[1:]
        if kind == RELAY:
            at, cross, index = where
            kinds = [3]
            if at <= unit < outer - 1:
                kinds.append(2)
            if at >= unit > 0:
                kinds.append(0)
            if not cross and (at == unit or not ROW_TURNS[index]):
                kinds.append(1)
            return [functools.partial(row_copy, unit, at, cross, index, way) for way in kinds[::-1]]
        if kind == AWAIT:
            at, index = where
            return [functools.partial(row_copy, unit, at, 1, index, 3)]
        if kind == TURN:
            return [functools.partial(turn_copy, *where)]
        if kind == CHAIN:
            return [functools.partial(chain_copy, *where, line + where[3] * step)]
        if kind == CROSS:
            return [functools.partial(cross_copy, unit, *where)]
        return []

    def arrivals(unit, cross, index):
        chip = block_of(unit, cross)
        sources = [part.at[chip, core], from_core.at[chip]]
        for sign, there in ((1, unit > 0), (-1, unit < outer - 1)):
            if there:
                chain_copy(unit, cross, index, sign, line).wait_recv()
                sources.append(chain_in.at[chain_slot(absolute(unit), line, sign), cross])
        return sources

    def run_task(unit, task):
        kind, where = task[0], task[1:]
        if kind == RELAY and (where[0] != unit or where[1]):
            row_copy(unit, where[0], where[1], where[2], 1).wait_recv()
        if kind == AWAIT:
            row_copy(unit, where[0], 1, where[1], 1).wait_recv()
        if kind == TURN:
            at, index = where
            chip = block_of(at, 1)
            add_up(part.at[chip, core], [part.at[chip, core], from_core.at[chip]], index)
        if kind == CHAIN:
            at, cross, index, sign = where
            chip = block_of(at, cross)
            sources = [part.at[chip, core], from_core.at[chip]]
            if PIECE_TURNS[index] and not cross:
                turn_copy(at, index).wait_recv()
                sources.append(turn_in.at[absolute(at)])
            if (unit if sign > 0 else outer - 1 - unit) > 0:
                chain_copy(at, cross, index, sign).wait_recv()
                sources.append(chain_in.at[absolute(at), cross])
            add_up(part.at[chip, core], sources, index)
        if kind == CROSS:
            sources = arrivals(unit, 1, where[0])
            add_up(part.at[block_of(unit, 1), core], sources, where[0])
        if kind == FINISH:
            index = where[0]
            sources = arrivals(unit, 0, index)
            if PIECE_TURNS[index]:
                turn_copy(unit, index).wait_recv()
                sources.append(turn_in.at[absolute(unit)])
            else:
                cross_copy(unit, index).wait_recv()
                sources.append(cross_in)
            add_up(out_ref, sources, index)
        for make in sends_of(unit, task):
            make().start()

    def all_sent(buf, blocks, extent, sem):
        if blocks * extent:
            sent = buf.at[pl.ds(0, blocks), core, pl.ds(0, extent)]
            pltpu.make_async_copy(sent, sent, sem).wait()

    def plan_of(unit):
        stretches, blocks, seen = [[]], [], set()
        for task in ORDERS[unit]:
            if task[0] == APPLY:
                blocks.append(task[1:])
                stretches.append([])
                continue
            need = {
                TURN: lambda: (task[1], 1),
                CHAIN: lambda: (task[1], task[2]),
                CROSS: lambda: (unit, 1),
                FINISH: lambda: (unit, 0),
            }.get(task[0], lambda: None)()
            fresh = need is not None and need not in seen
            seen.add(need)
            stretches[-1].append((task, need if fresh else None))
        return stretches, blocks

    plans = [plan_of(unit) for unit in range(len(ORDERS))]

    def run_stretch(unit, stretch):
        for task, fresh in stretch:
            if fresh is not None:
                half_copy(block_of(*fresh)).wait_recv()
            run_task(unit, task)

    def one_block(turn, carry):
        at = jnp.int32(0)
        cross = jnp.int32(0)
        for unit, (stretches, blocks) in enumerate(plans):
            for number, (block_at, block_cross) in enumerate(blocks):
                here = (place == unit) & (turn == number)
                at = jnp.where(here, block_at, at)
                cross = jnp.where(here, block_cross, cross)

                @pl.when(here)
                def _(unit=unit, stretch=stretches[number]):
                    run_stretch(unit, stretch)

        @pl.when(turn == 0)
        def _():
            for copy in copies[5:]:
                copy.wait()
            gate_t[...] = gate_w[...].T
            up_t[...] = up_w[...].T
            down_t[...] = down_w[...].T

        chip = chip_of(absolute(at), side + cross * (1 - 2 * side))
        slot = rows.at[chip, other]
        send(slot, slot, row_send.at[6], others_recv.at[chip], to_core).wait_recv()
        compute(chip)
        return carry

    lax.fori_loop(0, count, one_block, 0)
    for unit, (stretches, blocks) in enumerate(plans):
        @pl.when(place == unit)
        def _(unit=unit, stretches=stretches):
            run_stretch(unit, stretches[-1])
            turned_rows = sum(row_cuts[index][1] for index, flag in enumerate(ROW_TURNS) if flag)
            for kind, blocks in ((0, outer - unit if unit else 0), (2, unit + 1)):
                all_sent(rows, blocks, rows.shape[2], row_send.at[2 * kind])
                all_sent(rows, blocks, turned_rows, row_send.at[2 * kind + 1])
            all_sent(rows, 1, rows.shape[2], row_send.at[3])
            all_sent(rows, outer - 1, rows.shape[2] - turned_rows, row_send.at[2])

    first_rows = sum(piece_cuts[index][1] for index in turned_pieces)
    all_sent(rows, count, rows.shape[2], row_send.at[6])
    all_sent(part, count, feature_dim, half_send.at[0])
    all_sent(part, outer, first_rows, turn_send.at[0])
    all_sent(part, 1, feature_dim - first_rows, cross_send.at[0])
    all_sent(part, outer - 1, feature_dim, chain_send.at[0])
    all_sent(part, outer - 1, feature_dim - first_rows, chain_send.at[1])
    for index in range(len(proj_cuts)):
        proj_copy(index).wait_send()

    @pl.when(has_next == 1)
    def _():
        for copy in rims:
            copy.wait_send()


def hand_on(attended_ref, mixture_ref, attended_out, mixture_out, went):
    copies = [
        pltpu.make_async_copy(attended_ref, attended_out, went.at[0]),
        pltpu.make_async_copy(mixture_ref, mixture_out, went.at[1]),
    ]
    for copy in copies:
        copy.start()
    for copy in copies:
        copy.wait()


def whole_layer(
    queries, key_rows, values, sink_logit, o_weight, residual, norm_gain, routes, gate_codes,
    w_gate, w_up, w_down,
):
    row_count, feature_dim = residual.shape
    block_rows = row_count // 2
    chips = lax.axis_size("seq")
    outer = chips // INNER
    hidden_dim = w_gate.shape[2]
    turned = (feature_dim, block_rows)
    coded = (feature_dim + CODE_ROWS, block_rows)
    chunks, pieces = len(ROW_TURNS), len(PIECE_TURNS)
    dma = pltpu.SemaphoreType.DMA
    vmem = pl.BlockSpec(memory_space=pltpu.VMEM)
    half = jnp.bfloat16
    attended, mixture = pl.pallas_call(
        layer_kernel,
        out_shape=(pltpu.VMEM(turned, half), pltpu.VMEM(turned, half)),
        in_specs=[pl.BlockSpec(memory_space=pltpu.SMEM), vmem, vmem, vmem]
        + [pl.BlockSpec(memory_space=pl.ANY)] * 8,
        out_specs=(vmem, vmem),
        scratch_shapes=[
            pltpu.VMEM(queries.shape, half),
            pltpu.VMEM((WINDOW + row_count, key_rows.shape[1]), half),
            pltpu.VMEM((WINDOW + row_count, values.shape[1]), half),
            pltpu.VMEM(o_weight.shape[::-1], half),
            pltpu.VMEM(turned, half),
            pltpu.VMEM(queries.shape, half),
            pltpu.VMEM(turned, jnp.float32),
            pltpu.VMEM(turned, jnp.float32),
            pltpu.VMEM(turned, half),
            pltpu.VMEM(turned, half),
            dma((2,)),
            dma((2,)),
            dma((PROJ_CUTS,)),
            dma((PROJ_CUTS,)),
            pltpu.VMEM((chips, 2) + coded, half),
            pltpu.VMEM((chips, 2) + turned, half),
            pltpu.VMEM((chips,) + turned, half),
            pltpu.VMEM((outer + 1, 2) + turned, half),
            pltpu.VMEM((outer,) + turned, half),
            pltpu.VMEM(turned, half),
            pltpu.VMEM((feature_dim, hidden_dim), half),
            pltpu.VMEM((feature_dim, hidden_dim), half),
            pltpu.VMEM((hidden_dim, feature_dim), half),
            pltpu.VMEM((hidden_dim, feature_dim), half),
            pltpu.VMEM((hidden_dim, feature_dim), half),
            pltpu.VMEM((feature_dim, hidden_dim), half),
            dma((8,)),
            dma((chips, chunks)),
            dma((chips,)),
            dma((7,)),
            dma((1,)),
            dma((chips,)),
            dma((2,)),
            dma((outer + 1, 2 * pieces - sum(PIECE_TURNS))),
            dma((1,)),
            dma((outer, sum(PIECE_TURNS))),
            dma((1,)),
            dma((pieces - sum(PIECE_TURNS),)),
        ],
        compiler_params=pltpu.CompilerParams(
            collective_id=1, has_side_effects=True, vmem_limit_bytes=60 << 20
        ),
    )(
        sink_logit, norm_gain, routes.T, gate_codes.T, queries, key_rows, values,
        o_weight.T, residual.T, w_gate, w_up, w_down,
    )
    attended, mixture = pl.pallas_call(
        hand_on,
        out_shape=(jax.ShapeDtypeStruct(turned, half), jax.ShapeDtypeStruct(turned, half)),
        in_specs=[vmem] * 2,
        out_specs=(pl.BlockSpec(memory_space=pl.ANY),) * 2,
        scratch_shapes=[dma((2,))],
    )(*(pltpu.with_memory_space_constraint(value, pltpu.VMEM) for value in (attended, mixture)))
    return (attended.T, mixture.T)


def fits_kernel(queries, key_rows, residual, w_gate):
    chips = lax.axis_size("seq")
    return (
        lax.axis_size("exp") == 2
        and chips % INNER == 0
        and chips <= CODE_ROWS
        and residual.shape[1] % 16 == 0
        and chips == 2 * INNER * len(ORDERS)
        and w_gate.shape[0] == 1
        and residual.shape[0] == 2 * WINDOW
        and 2 * TOP >= chips
        and key_rows.shape[1] == LANES
        and queries.shape[1] % (2 * LANES) == 0
    )


def local(
    queries,
    key_rows,
    values,
    sink_logit,
    o_weight,
    residual,
    norm_gain,
    routes,
    gate_codes,
    w_gate,
    w_up,
    w_down,
):
    if fits_kernel(queries, key_rows, residual, w_gate):
        return whole_layer(
            queries, key_rows, values, sink_logit, o_weight, residual, norm_gain, routes,
            gate_codes, w_gate, w_up, w_down,
        )
    heads_out = window_attention(queries, key_rows, values, sink_logit)
    proj_terms = jnp.dot(heads_out, o_weight, preferred_element_type=jnp.float32)
    owners = lax.axis_size("exp")
    owner_pos = lax.axis_index("exp")
    block_rows = residual.shape[0] // owners
    expert_count = w_gate.shape[0] * lax.axis_size("seq")
    capacity = max(2, 2 * block_rows * TOP // expert_count)
    feature_dim = residual.shape[1]
    own_stream = lax.dynamic_slice_in_dim(residual, owner_pos * block_rows, block_rows, 0)
    own_routes = lax.dynamic_slice_in_dim(routes, owner_pos * block_rows, block_rows, 0)
    own_codes = lax.dynamic_slice_in_dim(gate_codes, owner_pos * block_rows, block_rows, 0)
    own_terms = lax.psum_scatter(proj_terms, "exp", scatter_dimension=0, tiled=True)
    attended = (own_stream.astype(jnp.float32) + own_terms).astype(jnp.bfloat16)
    normed = rms_norm(attended, norm_gain)
    outbox, pair_ids, within, shares = pack_rows(
        normed, own_routes, own_codes, expert_count, capacity
    )
    partial_value = expert_apply(
        lax.all_gather(
            lax.all_to_all(
                outbox.reshape(expert_count, capacity, feature_dim),
                "seq",
                split_axis=0,
                concat_axis=0,
                tiled=True,
            ),
            "exp",
            axis=0,
            tiled=True,
        ),
        w_gate,
        w_up,
        w_down,
    )
    whole = lax.psum_scatter(
        partial_value.astype(jnp.bfloat16), "exp", scatter_dimension=0, tiled=True
    ).astype(jnp.float32)
    returned = lax.all_to_all(
        whole.astype(jnp.bfloat16), "seq", split_axis=0, concat_axis=0, tiled=True
    ).astype(whole.dtype)
    picked = returned[pair_ids, within]
    mixture = jnp.sum((picked * shares[:, None]).reshape(-1, TOP, feature_dim), axis=1)
    return (attended, mixture.astype(jnp.bfloat16))


def solution(mesh):
    placed = (
        P(("groups", "seq"), "exp"),
        P(("groups", "seq"), "exp"),
        P(("groups", "seq"), "exp"),
        P("exp"),
        P("exp", None),
        P(("groups", "seq"), None),
        P(),
        P(("groups", "seq"), None),
        P(("groups", "seq"), None),
        P("seq", None, "exp"),
        P("seq", None, "exp"),
        P("seq", "exp", None),
    )
    return jax.shard_map(
        local,
        mesh=mesh,
        in_specs=placed,
        out_specs=(P(("groups", "seq", "exp"), None), P(("groups", "seq", "exp"), None)),
        check_vma=False,
    )
```
